32 devices in a mesh: half: 2 (over x), grid: 2 (over y), dom: 8 (over z, core).
Axes of the slice: x: 2, y: 2, z: 4, core: 2. Of those that a mesh axis runs over, the one named last changes fastest.
Arguments:
- grids: float32 [16, 64, 64, 4096], P(('half', 'grid'), 'dom'), may hold values from -0.8 to 0.8
- levels: int32 [16, 4], replicated, may hold values from 4 to 6, as said below
Outputs:
- combined: float32 [16, 64, 64, 4096], P(('half', 'grid'), 'dom')
The draws below stay inside these ranges and needn't reach their ends.
Inputs may be any that keep to these rules, and one draw needn't show every extreme that they name: `levels`: with base b = (4, 5, 5, 5), rows 0 to 7 are b plus, in some order, (2,1,1,0), (2,1,0,1), (2,0,1,1), (1,1,1,1), (1,1,0,0), (1,0,1,0), (1,0,0,1), (0,0,0,0); rows 8 to 15 are b plus, in some order, (2,1,0,0), (2,0,1,0), (2,0,0,1), (1,1,1,0), (1,1,0,1), (1,0,1,1), (2,0,0,0), (1,0,0,0).
All inputs are finite; a program needn't handle non-finite values.
Results may differ from the reference program's by a relative error of at most 0.0003.
Values sent between devices are 32-bit elements; how exact they have to be, the bound alone decides.
No kernel may reach another device: no remote copies, remote signals or barrier semaphores. Data moves between devices by JAX's collectives and lax.ppermute only.
A program may use at most 320 MiB of HBM per device.

```python
import jax
import jax.numpy as jnp
import numpy as np
from jax import lax

LEV1 = 6
LEV2 = 6
LEV3 = 6
LEV4 = 6
GRIDS = 16
N1 = 64
N2 = 64
N3 = 64
N4 = 64


def draw_levels(key, part):
    first_key, second_key = jax.random.split(jax.random.fold_in(key, 11), 2)
    first_half = jnp.array([[2, 1, 1, 0], [2, 1, 0, 1], [2, 0, 1, 1], [1, 1, 1, 1], [1, 1, 0, 0], [1, 0, 1, 0], [1, 0, 0, 1], [0, 0, 0, 0]], dtype=jnp.int32)
    second_half = jnp.array([[2, 1, 0, 0], [2, 0, 1, 0], [2, 0, 0, 1], [1, 1, 1, 0], [1, 1, 0, 1], [1, 0, 1, 1], [2, 0, 0, 0], [1, 0, 0, 0]], dtype=jnp.int32)
    first_half = first_half[jax.random.permutation(first_key, 8)]
    second_half = second_half[jax.random.permutation(second_key, 8)]
    lowest = jnp.array([LEV1 - 2, LEV2 - 1, LEV3 - 1, LEV4 - 1], dtype=jnp.int32)
    return (jnp.concatenate([first_half, second_half], axis=0) + lowest[None, :]).astype(jnp.int32)


def block_levels(own_key, dims, cuts, low, high):
    level, own = 1.0, jax.random.fold_in(own_key, 6)
    for position, blocks in cuts:
        draws = jnp.exp(jax.random.uniform(jax.random.fold_in(own, position), (blocks,), jnp.float32, low / len(cuts), high / len(cuts)))
        level = level * jnp.repeat(draws, dims[position] // blocks).reshape([-1 if axis == position else 1 for axis in range(len(dims))])
    return level


def gaussian(rng, extent, scale, reach, cuts=(), held_as=jnp.bfloat16):
    drawn = jax.random.normal(rng, extent, jnp.float32) * scale
    if len(cuts) > 0:
        drawn = block_levels(rng, extent, cuts, -0.22, 0.18) * drawn
    return jnp.clip(drawn, min=-reach, max=reach).astype(held_as)


def setup_inputs(seed: int = 0) -> dict:
    streams_of = jax.random.split(jax.random.key(seed), 3)
    return {
        "grids": gaussian(streams_of[0], (GRIDS, N1, N2, N3 * N4), 0.1, 0.8, ((0, 4), (1, 8)), jnp.float32),
        "levels": draw_levels(jax.random.fold_in(streams_of[2], 71), 0),
    }


HIGH = lax.Precision.HIGHEST
SPANS = (2, 1, 1, 1)


def level_ordering(level):
    points = 2 ** level
    ordering = [0]
    for section in range(1, level + 1):
        stride = 2 ** (level - section)
        ordering.extend(range(stride, points, 2 * stride))
    return np.array(ordering)


def hier_tables(level_top, spread):
    size_top = 2 ** level_top
    forwards = np.zeros((spread + 1, size_top, size_top))
    backwards = np.zeros((spread + 1, size_top, size_top))
    for offset in range(spread + 1):
        level = level_top - spread + offset
        points = 2 ** level
        down_rows = np.eye(points)
        up_rows = np.eye(points)
        for section in range(level, 0, -1):
            stride = 2 ** (level - section)
            odd_points = np.arange(stride, points, 2 * stride)
            down_rows[odd_points] = down_rows[odd_points] - 0.5 * (down_rows[odd_points - stride] + down_rows[(odd_points + stride) % points])
        for section in range(1, level + 1):
            stride = 2 ** (level - section)
            odd_points = np.arange(stride, points, 2 * stride)
            up_rows[odd_points] = up_rows[odd_points] + 0.5 * (up_rows[odd_points - stride] + up_rows[(odd_points + stride) % points])
        ordering = level_ordering(level)
        forwards[offset, :points, :points] = down_rows[ordering]
        backwards[offset, :points, :points] = up_rows[:, ordering]
    return jnp.asarray(forwards, jnp.float32), jnp.asarray(backwards, jnp.float32)


def combination_weights(levels):
    corners = np.array([[(corner >> place) & 1 for place in range(4)] for corner in range(16)], dtype=np.int32)
    parity = 1 - 2 * (corners.sum(axis=1) % 2)
    raised = levels[:, None, :] + jnp.asarray(corners, dtype=jnp.int32)[None, :, :]
    below = jnp.all(raised[:, :, None, :] <= levels[None, None, :, :], axis=3)
    inside = jnp.any(below, axis=2).astype(jnp.int32)
    return jnp.sum(inside * jnp.asarray(parity, dtype=jnp.int32)[None, :], axis=1)


def pick_tables(tables, level_column, level_top, spread):
    shifted = (level_column - (level_top - spread)).astype(jnp.int32)
    onehot = (jnp.arange(spread + 1, dtype=jnp.int32)[None, :] == shifted[:, None]).astype(jnp.float32)
    return jnp.einsum('gs,sij->gij', onehot, tables, precision=HIGH)


def transform(values, matrices):
    values = jnp.einsum('ai,ibcd->abcd', matrices[0], values, precision=HIGH)
    values = jnp.einsum('bi,aicd->abcd', matrices[1], values, precision=HIGH)
    values = jnp.einsum('ci,abid->abcd', matrices[2], values, precision=HIGH)
    values = jnp.einsum('di,abci->abcd', matrices[3], values, precision=HIGH)
    return values


def reference(grids, levels):
    finest = [LEV1, LEV2, LEV3, LEV4]
    table_sets = [hier_tables(finest[axis_index], SPANS[axis_index]) for axis_index in range(4)]
    weights = combination_weights(levels).astype(jnp.float32)

    def accumulate(running, items):
        grid, level_row, weight = items
        matrices = [pick_tables(table_sets[axis_index][0], level_row[axis_index:axis_index + 1], finest[axis_index], SPANS[axis_index])[0] for axis_index in range(4)]
        surplus = transform(grid.reshape(N1, N2, N3, N4), matrices)
        return running + weight * surplus, None

    totals, unused = lax.scan(accumulate, jnp.zeros((N1, N2, N3, N4), jnp.float32), (grids, levels, weights))

    def expand(level_row):
        matrices = [pick_tables(table_sets[axis_index][1], level_row[axis_index:axis_index + 1], finest[axis_index], SPANS[axis_index])[0] for axis_index in range(4)]
        return transform(totals, matrices).reshape(N1, N2, N3 * N4)

    return lax.map(expand, levels)
```

```python
import jax
import jax.numpy as jnp
import numpy as np
from jax import lax
from jax.experimental import pallas as pl
from jax.experimental.pallas import tpu as pltpu
from jax.sharding import PartitionSpec as P

LEV1 = 6
LEV2 = 6
LEV3 = 6
LEV4 = 6
N1 = 64
N2 = 64
N3 = 64
N4 = 64
SPANS = (2, 1, 1, 1)


BLOCKS = (
    (0, 0, 0), (1, 0, 0), (0, 1, 0), (0, 0, 1),
    (1, 1, 0), (1, 0, 1), (0, 1, 1), (1, 1, 1),
)
WHERE = {block: place for place, block in enumerate(BLOCKS)}
SHARED_D = 4
SHARED_C = 7
HB = N2 // 2
HC = N3 // 2
HD = N4 // 2
GROUPS = 8
CG = N3 // GROUPS
LANES = HC * HD
HALF_LANES = LANES // 2
QR = HB // 4
TILE = CG // 2 * HD
SLOTS = tuple((h, sx, sy) for h in range(2) for sx in range(2) for sy in range(2))


def combination_weights(levels):
    corners = np.array(
        [[corner >> place & 1 for place in range(4)] for corner in range(16)], dtype=np.int32
    )
    parity = 1 - 2 * (corners.sum(axis=1) % 2)
    raised = levels[:, None, :] + jnp.asarray(corners, dtype=jnp.int32)[None, :, :]
    below = jnp.all(raised[:, :, None, :] <= levels[None, None, :, :], axis=3)
    inside = jnp.any(below, axis=2).astype(jnp.int32)
    return jnp.sum(inside * jnp.asarray(parity, dtype=jnp.int32)[None, :], axis=1)


def split_matrix(fine_in, count_in, half, wrap):
    table = np.zeros((count_in, 2, half))
    for k in range(half):
        table[2 * k, 0, k] = 1.0
        table[2 * k + 1, 1, k] += 1.0
        table[2 * k, 1, k] -= 0.5
        table[(2 * k + 2) % wrap, 1, k] -= 0.5
    return table


def plain_matrix(count_in, half):
    table = np.zeros((count_in, 1, half))
    for k in range(half):
        table[k, 0, k] = 1.0
    return table


def join_matrix(parts_in, half_out, wrap, next_points):
    table = np.zeros((parts_in, half_out + next_points, 2 * half_out))
    for k in range(half_out):
        table[0, k, 2 * k] = 1.0
        table[1, k, 2 * k + 1] += 1.0
        table[0, k, 2 * k + 1] += 0.5
        table[0, (k + 1) % wrap, 2 * k + 1] += 0.5
    return table


def forward_tables():
    half_c = CG // 2
    tables = {}
    for oc in range(2):
        for od in range(2):
            if oc:
                along_c = split_matrix(True, CG + 2, half_c, CG + 2)
            else:
                along_c = plain_matrix(half_c, half_c)
            along_d = split_matrix(True, N4, HD, N4) if od else plain_matrix(N4, HD)
            table = np.einsum("cpk,dql->cdpqkl", along_c, along_d)
            rows = along_c.shape[0] * N4
            tables[oc, od] = jnp.asarray(table.reshape(rows, -1), jnp.bfloat16)
    return tables


def backward_tables():
    half_c = CG // 2
    tables = {}
    for oc in range(2):
        for od in range(2):
            if od:
                along_d = join_matrix(2, HD, HD, 0)
            else:
                along_d = np.zeros((1, HD, N4))
                along_d[0, np.arange(HD), np.arange(HD)] = 1.0
            if oc:
                along_c = join_matrix(2, half_c, half_c + half_c, half_c)
                own = np.einsum("pkc,qld->pqklcd", along_c[:, :half_c], along_d)
                ahead = np.einsum("pkc,qld->pqklcd", along_c[:1, half_c:], along_d)
                cols = CG * N4
                table = np.concatenate([own.reshape(-1, cols), ahead.reshape(-1, cols)], axis=0)
            else:
                along_c = np.eye(half_c)[None]
                table = np.einsum("pkc,qld->pqklcd", along_c, along_d).reshape(-1, half_c * N4)
            tables[oc, od] = jnp.asarray(table, jnp.bfloat16)
    return tables


CASES = ((0, 0), (0, 1), (1, 0), (1, 1))


def split_parts(value):
    high = value.astype(jnp.bfloat16)
    low = (value - high.astype(jnp.float32)).astype(jnp.bfloat16)
    return high, low


def forward_kernel(rows_here, count, scal, weight, x_ref, *refs):
    tables = dict(zip(CASES, refs[:4]))
    outs = refs[4:-2]
    xb, yb = refs[-2:]
    s5 = dict(zip(SLOTS, outs[0:8]))
    e6 = dict(zip(SLOTS, outs[8:16]))
    d6 = dict(zip(SLOTS, outs[16:24]))
    s5_self, d6_self, s4 = outs[24:27]
    i = pl.program_id(0)
    g = pl.program_id(1)
    level = scal[4 * g]
    fine_b = scal[4 * g + 1]
    fine_c = scal[4 * g + 2]
    fine_d = scal[4 * g + 3]
    mine_x = scal[4 * count]
    mine_y = scal[4 * count + 1]
    row = scal[4 * count + 2] + i
    odd = lax.rem(i, 2) == 1
    even = lax.rem(i, 2) == 0

    @pl.when(g == 0)
    def _():
        for slot in SLOTS:
            s5[slot][...] = jnp.zeros_like(s5[slot])
        s5_self[...] = jnp.zeros_like(s5_self)
        s4[...] = jnp.zeros_like(s4)

    @pl.when((g == 0) & even)
    def _():
        for slot in SLOTS:
            e6[slot][...] = jnp.zeros_like(e6[slot])

    @pl.when((g == 0) & odd)
    def _():
        for slot in SLOTS:
            d6[slot][...] = jnp.zeros_like(d6[slot])
        d6_self[...] = jnp.zeros_like(d6_self)

    active = row < (N1 // 4) * (1 << level)

    def put(values, fine_c_here):
        rows = slice(0, values.shape[0])
        high, low = split_parts(values)
        span = CG * N4 if fine_c_here else CG // 2 * N4
        reach = span + 2 * N4 if fine_c_here else span
        for k in range(GROUPS):
            for place, piece in ((0, high), (reach, low)):
                xb[k, rows, place : place + span] = piece[:, k * span : k * span + span]
                if fine_c_here:
                    ahead = (k + 1) % GROUPS * span
                    xb[k, rows, place + span : place + reach] = piece[:, ahead : ahead + 2 * N4]

    for oc, od in CASES:
        for ob in range(2):
            @pl.when(active & (fine_b == ob) & (fine_c == oc) & (fine_d == od))
            def _(oc=oc, od=od, ob=ob):
                lanes = N3 * N4 if oc else HC * N4
                rows = (1 + ob) * HB
                put(x_ref[0, 0, :rows, :lanes], oc)
                reach = (CG + 2) * N4 if oc else CG // 2 * N4
                table = tables[oc, od][...]
                lhs = xb[:, :rows, : 2 * reach].reshape(GROUPS * rows, 2 * reach)
                result = jnp.dot(
                    lhs[:, :reach], table, preferred_element_type=jnp.float32
                ) + jnp.dot(lhs[:, reach:], table, preferred_element_type=jnp.float32)
                for pc in range(oc + 1):
                    for pd in range(od + 1):
                        column = (pc * (od + 1) + pd) * TILE
                        for k in range(GROUPS):
                            piece = result[k * rows : k * rows + rows, column : column + TILE]
                            if ob:
                                yb[2 * pc + pd, k, :N2] = piece
                                yb[2 * pc + pd, k, N2:] = piece[:QR]
                            else:
                                yb[2 * pc + pd, k, pl.ds(0, HB, stride=2)] = piece

    scale = weight[g]

    def add_up(wanted, blocks, target):
        for block in blocks:
            pb, pc, pd = BLOCKS[block]

            @pl.when(wanted & (pb <= fine_b) & (pc <= fine_c) & (pd <= fine_d))
            def _(block=block, pb=pb, part=2 * pc + pd):
                for h, sx, sy in SLOTS:
                    quarter = 2 * (sx ^ mine_x) + (sy ^ mine_y)
                    start = pl.multiple_of(quarter * 2 * QR, 2 * QR)
                    ref, index = target(block, h, sx, sy)
                    for j in range(GROUPS // 2):
                        k = h * (GROUPS // 2) + j
                        piece = yb[part, k, pl.ds(start, QR, stride=2)]
                        if pb:
                            piece = yb[part, k, pl.ds(start + 1, QR, stride=2)] - 0.5 * (
                                piece + yb[part, k, pl.ds(start + 2, QR, stride=2)]
                            )
                        where = index + (slice(None), slice(j * TILE, j * TILE + TILE))
                        ref[where] += scale * piece

    add_up(
        active & (level == 2) & even,
        range(SHARED_C),
        lambda block, h, sx, sy: (e6[h, sx, sy], (block, 0)),
    )
    add_up(
        active & (level == 2) & odd,
        range(SHARED_D),
        lambda block, h, sx, sy: (d6[h, sx, sy], (block, 0)),
    )
    add_up(
        active & (level == 2) & odd,
        range(SHARED_D, SHARED_C),
        lambda block, h, sx, sy: (d6_self, (h, sx, sy, block - SHARED_D, 0)),
    )
    add_up(
        active & (level == 1),
        range(SHARED_C),
        lambda block, h, sx, sy: (s5[h, sx, sy], (block, 0)),
    )
    add_up(
        active & (level == 1),
        range(SHARED_C, 8),
        lambda block, h, sx, sy: (s5_self, (h, sx, sy, 0)),
    )
    add_up(
        active & (level == 0),
        range(1),
        lambda block, h, sx, sy: (s4, (h, sx, sy, 0)),
    )

    @pl.when((g == count - 1) & (i > 0))
    def _():
        for h, sx, sy in SLOTS:
            d6[h, sx, sy][...] -= 0.5 * e6[h, sx, sy][:SHARED_D]
            d6_self[h, sx, sy] -= 0.5 * e6[h, sx, sy][SHARED_D:]


def forward(grids, scal, weight):
    count, rows_here = grids.shape[:2]
    half_rows = rows_here // 2
    tables = forward_tables()

    def constant(table):
        return pl.BlockSpec(table.shape, lambda i, g, *_: (0, 0))

    def rows_spec(blocks, row_of):
        return pl.BlockSpec(
            (blocks, 1, QR, HALF_LANES), lambda i, g, *_: (0, row_of(i), 0, 0)
        )

    def self_spec(blocks, row_of):
        if blocks is None:
            return pl.BlockSpec(
                (2, 2, 2, 1, QR, HALF_LANES), lambda i, g, *_: (0, 0, 0, row_of(i), 0, 0)
            )
        return pl.BlockSpec(
            (2, 2, 2, blocks, 1, QR, HALF_LANES), lambda i, g, *_: (0, 0, 0, 0, row_of(i), 0, 0)
        )

    def shape(*dims):
        return jax.ShapeDtypeStruct(dims + (QR, HALF_LANES), jnp.float32)

    def even_row(i):
        return i // 2

    def odd_row(i):
        return jnp.maximum(i - 1, 0) // 2

    out_specs = (
        [rows_spec(SHARED_C, lambda i: i)] * 8
        + [rows_spec(SHARED_C, even_row)] * 8
        + [rows_spec(SHARED_D, odd_row)] * 8
        + [
            self_spec(None, lambda i: i),
            self_spec(SHARED_C - SHARED_D, odd_row),
            self_spec(None, lambda i: i),
        ]
    )
    out_shape = (
        [shape(SHARED_C, rows_here)] * 8
        + [shape(SHARED_C, half_rows)] * 8
        + [shape(SHARED_D, half_rows)] * 8
        + [
            shape(2, 2, 2, rows_here),
            shape(2, 2, 2, SHARED_C - SHARED_D, half_rows),
            shape(2, 2, 2, rows_here),
        ]
    )
    ordered = [tables[case] for case in CASES]
    outs = pl.pallas_call(
        lambda *refs: forward_kernel(rows_here, count, *refs),
        grid_spec=pltpu.PrefetchScalarGridSpec(
            num_scalar_prefetch=2,
            grid=(rows_here, count),
            in_specs=[pl.BlockSpec((1, 1, N2, N3 * N4), lambda i, g, *_: (g, i, 0, 0))]
            + [constant(table) for table in ordered],
            out_specs=out_specs,
            scratch_shapes=[
                pltpu.VMEM((GROUPS, 2 * HB, 2 * (CG + 2) * N4), jnp.bfloat16),
                pltpu.VMEM((4, GROUPS, N2 + QR, TILE), jnp.float32),
            ],
        ),
        out_shape=out_shape,
        compiler_params=pltpu.CompilerParams(vmem_limit_bytes=48 * 2**20),
        name="split_grids",
    )(scal, weight, grids, *ordered)
    s5 = dict(zip(SLOTS, outs[0:8]))
    e6 = dict(zip(SLOTS, outs[8:16]))
    d6 = dict(zip(SLOTS, outs[16:24]))
    return (s5, e6, d6) + tuple(outs[24:])


def backward_kernel(rows_here, count, scal, *refs):
    c6a, c6b, d6, d6_self, c5, s5_self, c4 = refs[:7]
    tables = dict(zip(CASES, refs[7:11]))
    out = refs[11]
    coarse, detail, joined, xb = refs[12:]
    i = pl.program_id(0)
    g = pl.program_id(1)
    level = scal[4 * g]
    fine_b = scal[4 * g + 1]
    fine_c = scal[4 * g + 2]
    fine_d = scal[4 * g + 3]
    mine_x = scal[4 * count]
    mine_y = scal[4 * count + 1]
    row = scal[4 * count + 2] + i
    odd = lax.rem(i, 2) == 1
    even = lax.rem(i, 2) == 0
    active = row < (N1 // 4) * (1 << level)

    def stage(wanted, blocks, source):
        for block in blocks:
            pb, pc, pd = BLOCKS[block]

            @pl.when(active & wanted & (pb <= fine_b) & (pc <= fine_c) & (pd <= fine_d))
            def _(block=block, work=(coarse, detail)[pb], part=2 * pc + pd):
                for h, sx, sy in SLOTS:
                    quarter = 2 * (sx ^ mine_x) + (sy ^ mine_y)
                    start = pl.multiple_of(quarter * QR, QR)
                    value = source(block, h, sx, sy)
                    for j in range(GROUPS // 2):
                        k = h * (GROUPS // 2) + j
                        work[part, k, pl.ds(start, QR)] = value[:, j * TILE : j * TILE + TILE]

    def between(block, h, sx, sy):
        mean = 0.5 * (c6a[h, sx, sy, block, 0] + c6b[h, sx, sy, block, 0])
        if block < SHARED_D:
            return mean + d6[h, sx, sy, block, 0]
        return mean + d6_self[h, sx, sy, block - SHARED_D, 0]

    stage((level == 2) & even, range(SHARED_C), lambda b, h, x, y: c6a[h, x, y, b, 0])
    stage((level == 2) & odd, range(SHARED_C), between)
    stage(level == 1, range(SHARED_C), lambda b, h, x, y: c5[h, x, y, b, 0])
    stage(level == 1, range(SHARED_C, 8), lambda b, h, x, y: s5_self[h, x, y, 0])
    stage(level == 0, range(1), lambda b, h, x, y: c4[h, x, y, 0])

    @pl.when(jnp.logical_not(active))
    def _():
        out[...] = jnp.zeros_like(out)

    for oc, od in CASES:
        for ob in range(2):
            @pl.when(active & (fine_b == ob) & (fine_c == oc) & (fine_d == od))
            def _(oc=oc, od=od, ob=ob):
                parts = [(pc, pd) for pc in range(oc + 1) for pd in range(od + 1)]
                ahead = [(0, pd) for pd in range(od + 1)] if oc else []
                reach = (len(parts) + len(ahead)) * TILE
                rows = (1 + ob) * HB
                for place, (pc, pd) in enumerate(parts):
                    part = 2 * pc + pd
                    for k in range(GROUPS):
                        value = coarse[part, k, :HB]
                        if ob:
                            coarse[part, k, HB:] = coarse[part, k, :QR]
                            mean = 0.5 * (value + coarse[part, k, 1 : HB + 1])
                            joined[k, pl.ds(0, HB, stride=2)] = value
                            joined[k, pl.ds(1, HB, stride=2)] = detail[part, k] + mean
                            value = joined[k]
                        for base, piece in zip((0, reach), split_parts(value)):
                            start = base + place * TILE
                            xb[k, :rows, start : start + TILE] = piece
                            if oc and not pc:
                                start = base + (len(parts) + pd) * TILE
                                before = (k + GROUPS - 1) % GROUPS
                                xb[before, :rows, start : start + TILE] = piece
                table = tables[oc, od][...]
                lhs = xb[:, :rows, : 2 * reach].reshape(GROUPS * rows, 2 * reach)
                result = jnp.dot(
                    lhs[:, :reach], table, preferred_element_type=jnp.float32
                ) + jnp.dot(lhs[:, reach:], table, preferred_element_type=jnp.float32)
                span = CG * N4 if oc else CG // 2 * N4
                for k in range(GROUPS):
                    out[0, 0, :rows, k * span : k * span + span] = result[
                        k * rows : k * rows + rows
                    ]
                if not ob:
                    out[0, 0, HB:, :] = jnp.zeros((HB, N3 * N4), jnp.float32)
                if not oc:
                    out[0, 0, :, HC * N4 :] = jnp.zeros((N2, HC * N4), jnp.float32)


def backward(count, scal, c6, d6, d6_self, c5, s5_self, c4):
    rows_here = c5.shape[4]
    tables = backward_tables()
    ordered = [tables[case] for case in CASES]

    def constant(table):
        return pl.BlockSpec(table.shape, lambda i, g, *_: (0, 0))

    def spec(blocks, row_of):
        return pl.BlockSpec(
            (2, 2, 2, blocks, 1, QR, HALF_LANES), lambda i, g, *_: (0, 0, 0, 0, row_of(i), 0, 0)
        )

    def line_spec(row_of):
        return pl.BlockSpec(
            (2, 2, 2, 1, QR, HALF_LANES), lambda i, g, *_: (0, 0, 0, row_of(i), 0, 0)
        )

    return pl.pallas_call(
        lambda *refs: backward_kernel(rows_here, count, *refs),
        grid_spec=pltpu.PrefetchScalarGridSpec(
            num_scalar_prefetch=1,
            grid=(rows_here, count),
            in_specs=[
                spec(SHARED_C, lambda i: i // 2),
                spec(SHARED_C, lambda i: (i + 1) // 2),
                spec(SHARED_D, lambda i: i // 2),
                spec(SHARED_C - SHARED_D, lambda i: i // 2),
                spec(SHARED_C, lambda i: i),
                line_spec(lambda i: i),
                line_spec(lambda i: i),
            ]
            + [constant(table) for table in ordered],
            out_specs=pl.BlockSpec((1, 1, N2, N3 * N4), lambda i, g, *_: (g, i, 0, 0)),
            scratch_shapes=[
                pltpu.VMEM((4, GROUPS, HB + QR, TILE), jnp.float32),
                pltpu.VMEM((4, GROUPS, HB, TILE), jnp.float32),
                pltpu.VMEM((GROUPS, N2, TILE), jnp.float32),
                pltpu.VMEM((GROUPS, N2, 12 * TILE), jnp.bfloat16),
            ],
        ),
        out_shape=jax.ShapeDtypeStruct((count, rows_here, N2, N3 * N4), jnp.float32),
        compiler_params=pltpu.CompilerParams(vmem_limit_bytes=48 * 2**20),
        name="join_grids",
    )(scal, c6, c6, d6, d6_self, c5, s5_self, c4, *ordered)


def stack_slots(pieces):
    return jnp.stack(
        [
            jnp.stack([jnp.stack([pieces[h, sx, sy] for sy in range(2)]) for sx in range(2)])
            for h in range(2)
        ]
    )


def exchange(value, axis, domains):
    dom_count = lax.axis_size("dom")
    pairs = []
    for x in range(2):
        for y in range(2):
            other = (1 - x, y) if axis == "half" else (x, 1 - y)
            for d in range(domains):
                pairs.append(
                    ((x * 2 + y) * dom_count + d, (other[0] * 2 + other[1]) * dom_count + d)
                )
    return lax.ppermute(value, ("half", "grid", "dom"), pairs)


def reduce_quarter(pieces, domains):
    reduced = []
    for h in range(2):
        first, second = (("half", "grid"), ("grid", "half"))[h]
        far = lambda a, b: pieces[(h, a, b) if h == 0 else (h, b, a)]
        onward = far(0, 1) + exchange(far(1, 1), first, domains)
        nearby = far(0, 0) + exchange(far(1, 0), first, domains)
        reduced.append(nearby + exchange(onward, second, domains))
    return jnp.stack(reduced)


def gather_quarters(own, domains):
    pieces = {}
    for h in range(2):
        first, second = (("half", "grid"), ("grid", "half"))[h]
        place = lambda a, b: (h, a, b) if h == 0 else (h, b, a)
        pieces[place(0, 0)] = own[h]
        pieces[place(0, 1)] = exchange(own[h], second, domains)
        pieces[place(1, 0)] = exchange(own[h], first, domains)
        pieces[place(1, 1)] = exchange(pieces[place(0, 1)], first, domains)
    return stack_slots(pieces)


def rows_up(value):
    half_rows = value.shape[-3] // 2
    sources = lax.axis_size("dom") // 2
    low = lax.ppermute(value[..., :half_rows, :, :], "dom", [(d, 2 * d) for d in range(sources)])
    high = lax.ppermute(
        value[..., half_rows:, :, :], "dom", [(d, 2 * d + 1) for d in range(sources)]
    )
    return low + high


def rows_down(value):
    targets = lax.axis_size("dom") // 2
    low = lax.ppermute(value, "dom", [(2 * d, d) for d in range(targets)])
    high = lax.ppermute(value, "dom", [(2 * d + 1, d) for d in range(targets)])
    return jnp.concatenate([low, high], axis=-3)


def next_row(value, devices):
    return lax.ppermute(
        value[..., :1, :, :], "dom", [((d + 1) % devices, d) for d in range(devices)]
    )


def per_device(grids, levels):
    count, rows_here = grids.shape[:2]
    half_rows = rows_here // 2
    half_size = lax.axis_size("half")
    grid_size = lax.axis_size("grid")
    dom_size = lax.axis_size("dom")
    square = half_size == 2 and grid_size == 2
    group = lax.axis_index("half") * grid_size + lax.axis_index("grid")
    weights = combination_weights(levels).astype(jnp.float32)
    lowest = jnp.array(
        [LEV1 - SPANS[0], LEV2 - SPANS[1], LEV3 - SPANS[2], LEV4 - SPANS[3]], dtype=jnp.int32
    )
    offsets = levels - lowest[None, :]
    own_offsets = lax.dynamic_slice_in_dim(offsets, group * count, count, 0)
    own_weights = lax.dynamic_slice_in_dim(weights, group * count, count, 0)
    zero = jnp.zeros((), jnp.int32)
    place = jnp.stack(
        [
            lax.axis_index("half") if square else zero,
            lax.axis_index("grid") if square else zero,
            lax.axis_index("dom") * rows_here,
        ]
    ).astype(jnp.int32)
    scal = jnp.concatenate([own_offsets.reshape(-1), place])
    s5, e6, d6, s5_self, d6_self, s4 = forward(grids, scal, own_weights)

    s4 = s4[:, :, :, None]
    ahead = next_row(s4, dom_size // 4)
    longer = jnp.concatenate([s4, ahead], axis=-3)
    mids = 0.5 * (longer[..., :-1, :, :] + longer[..., 1:, :, :])
    spread = jnp.stack([s4, mids], axis=-3).reshape(
        s4.shape[:-3] + (2 * rows_here,) + s4.shape[-2:]
    )
    quarter_devices = dom_size // 4
    low = lax.ppermute(
        spread[..., :rows_here, :, :], "dom", [(d, 2 * d) for d in range(quarter_devices)]
    )
    high = lax.ppermute(
        spread[..., rows_here:, :, :], "dom", [(d, 2 * d + 1) for d in range(quarter_devices)]
    )
    coarsest = rows_up(low + high)

    firsts = stack_slots({slot: e6[slot][:, :1] for slot in SLOTS})
    e6_ahead = next_row(firsts, dom_size)
    d6_self = d6_self.at[..., -1:, :, :].add(-0.5 * e6_ahead[:, :, :, SHARED_D:])
    d6 = {
        slot: d6[slot].at[:, -1:].add(-0.5 * e6_ahead[slot][:SHARED_D]) for slot in SLOTS
    }
    e6 = {slot: e6[slot].at[:1].add(coarsest[slot]) for slot in SLOTS}

    if square:
        s5_own = reduce_quarter(s5, dom_size // 2)
        e6_own = reduce_quarter(e6, dom_size)
        d6_own = reduce_quarter(d6, dom_size)
    else:
        s5_own, e6_own, d6_own = lax.psum(
            (stack_slots(s5), stack_slots(e6), stack_slots(d6)), ("half", "grid")
        )
    c6_own = e6_own + rows_up(s5_own)
    c5_own = rows_down(c6_own)
    c6_own = jnp.concatenate([c6_own, next_row(c6_own, dom_size)], axis=-3)
    evens = c5_own[..., :1, ::2, :, :]
    c4_own = rows_down(evens)
    c5_own = jnp.concatenate([c5_own, c4_own], axis=-4)
    if square:
        d6 = gather_quarters(d6_own, dom_size)
        c6 = gather_quarters(c6_own, dom_size)
        c5 = gather_quarters(c5_own, dom_size // 2)
    else:
        c5, c6, d6 = c5_own, c6_own, d6_own
    return backward(
        count, scal, c6, d6, d6_self, c5, s5_self, c5[:, :, :, SHARED_C]
    )


def solution(mesh):
    return jax.shard_map(
        per_device,
        mesh=mesh,
        in_specs=(P(("half", "grid"), "dom", None, None), P()),
        out_specs=P(("half", "grid"), "dom", None, None),
        check_vma=False,
    )
```

```python
import jax
import jax.numpy as jnp
import numpy as np
from jax import lax
from jax.experimental import pallas as pl
from jax.experimental.pallas import tpu as pltpu
from jax.sharding import PartitionSpec as P

LEV1 = 6
LEV2 = 6
LEV3 = 6
LEV4 = 6
N1 = 64
N2 = 64
N3 = 64
N4 = 64
SPANS = (2, 1, 1, 1)


BLOCKS = (
    (0, 0, 0), (1, 0, 0), (0, 1, 0), (0, 0, 1),
    (1, 1, 0), (1, 0, 1), (0, 1, 1), (1, 1, 1),
)
WHERE = {block: place for place, block in enumerate(BLOCKS)}
SHARED_D = 4
SHARED_C = 7
HB = N2 // 2
HC = N3 // 2
HD = N4 // 2
GROUPS = 8
CG = N3 // GROUPS
LANES = HC * HD
HALF_LANES = LANES // 2
QR = HB // 4
TILE = CG // 2 * HD
SLOTS = tuple((h, sx, sy) for h in range(2) for sx in range(2) for sy in range(2))


def combination_weights(levels):
    corners = np.array(
        [[corner >> place & 1 for place in range(4)] for corner in range(16)], dtype=np.int32
    )
    parity = 1 - 2 * (corners.sum(axis=1) % 2)
    raised = levels[:, None, :] + jnp.asarray(corners, dtype=jnp.int32)[None, :, :]
    below = jnp.all(raised[:, :, None, :] <= levels[None, None, :, :], axis=3)
    inside = jnp.any(below, axis=2).astype(jnp.int32)
    return jnp.sum(inside * jnp.asarray(parity, dtype=jnp.int32)[None, :], axis=1)


def split_matrix(fine_in, count_in, half, wrap):
    table = np.zeros((count_in, 2, half))
    for k in range(half):
        table[2 * k, 0, k] = 1.0
        table[2 * k + 1, 1, k] += 1.0
        table[2 * k, 1, k] -= 0.5
        table[(2 * k + 2) % wrap, 1, k] -= 0.5
    return table


def plain_matrix(count_in, half):
    table = np.zeros((count_in, 1, half))
    for k in range(half):
        table[k, 0, k] = 1.0
    return table


def join_matrix(parts_in, half_out, wrap, next_points):
    table = np.zeros((parts_in, half_out + next_points, 2 * half_out))
    for k in range(half_out):
        table[0, k, 2 * k] = 1.0
        table[1, k, 2 * k + 1] += 1.0
        table[0, k, 2 * k + 1] += 0.5
        table[0, (k + 1) % wrap, 2 * k + 1] += 0.5
    return table


def forward_tables():
    half_c = CG // 2
    tables = {}
    for oc in range(2):
        for od in range(2):
            if oc:
                along_c = split_matrix(True, CG + 2, half_c, CG + 2)
            else:
                along_c = plain_matrix(half_c, half_c)
            along_d = split_matrix(True, N4, HD, N4) if od else plain_matrix(N4, HD)
            table = np.einsum("cpk,dql->cdpqkl", along_c, along_d)
            rows = along_c.shape[0] * N4
            tables[oc, od] = jnp.asarray(table.reshape(rows, -1), jnp.bfloat16)
    return tables


def backward_tables():
    half_c = CG // 2
    tables = {}
    for oc in range(2):
        for od in range(2):
            if od:
                along_d = join_matrix(2, HD, HD, 0)
            else:
                along_d = np.zeros((1, HD, N4))
                along_d[0, np.arange(HD), np.arange(HD)] = 1.0
            if oc:
                along_c = join_matrix(2, half_c, half_c + half_c, half_c)
                own = np.einsum("pkc,qld->pqklcd", along_c[:, :half_c], along_d)
                ahead = np.einsum("pkc,qld->pqklcd", along_c[:1, half_c:], along_d)
                cols = CG * N4
                table = np.concatenate([own.reshape(-1, cols), ahead.reshape(-1, cols)], axis=0)
            else:
                along_c = np.eye(half_c)[None]
                table = np.einsum("pkc,qld->pqklcd", along_c, along_d).reshape(-1, half_c * N4)
            tables[oc, od] = jnp.asarray(table, jnp.bfloat16)
    return tables


CASES = ((0, 0), (0, 1), (1, 0), (1, 1))


def split_parts(value):
    high = value.astype(jnp.bfloat16)
    low = (value - high.astype(jnp.float32)).astype(jnp.bfloat16)
    return high, low


def grid_facts(count, scal, g):
    return tuple(scal[4 * g + axis] for axis in range(4))


def forward_kernel(fine, rows_here, count, scal, fetch, weight, x_ref, *refs):
    tables = dict(zip(CASES, refs[:4]))
    outs = refs[4:-2]
    xb, yb = refs[-2:]
    half_rows = rows_here // 2
    i = pl.program_id(0)
    g = pl.program_id(1)
    level, fine_b, fine_c, fine_d = grid_facts(count, scal, g)
    mine_x = scal[4 * count]
    mine_y = scal[4 * count + 1]
    row = scal[4 * count + 2] + i
    odd = lax.rem(i, 2) == 1
    even = lax.rem(i, 2) == 0
    active = row < (N1 // 4) * (1 << level)
    active = active & ((level == 2) if fine else (level < 2))

    def clear(wanted, *targets):
        @pl.when((g == 0) & wanted)
        def _():
            for target in targets:
                target[...] = jnp.zeros_like(target)

    if fine:
        e6 = dict(zip(SLOTS, outs[:8]))
        d6 = dict(zip(SLOTS, outs[8:16]))
        e6_rest, d6_self = outs[16:]
        clear(even, *outs[:8], e6_rest)
        clear(odd, *outs[8:16], d6_self)
    else:
        s5 = dict(zip(SLOTS, outs[:8]))
        s5_low, s5_high, s5_self, s4 = outs[8:]
        clear(i >= 0, *outs[:8], s5_self, s4)
        clear(i < half_rows, s5_low)
        clear(i >= half_rows, s5_high)

    def put(values, fine_c_here):
        rows = slice(0, values.shape[0])
        high, low = split_parts(values)
        span = CG * N4 if fine_c_here else CG // 2 * N4
        reach = span + 2 * N4 if fine_c_here else span
        for k in range(GROUPS):
            for place, piece in ((0, high), (reach, low)):
                xb[k, rows, place : place + span] = piece[:, k * span : k * span + span]
                if fine_c_here:
                    ahead = (k + 1) % GROUPS * span
                    xb[k, rows, place + span : place + reach] = piece[:, ahead : ahead + 2 * N4]

    for oc, od in CASES:
        for ob in range(2):
            @pl.when(active & (fine_b == ob) & (fine_c == oc) & (fine_d == od))
            def _(oc=oc, od=od, ob=ob):
                lanes = N3 * N4 if oc else HC * N4
                rows = (1 + ob) * HB
                put(x_ref[0, 0, :rows, :lanes], oc)
                reach = (CG + 2) * N4 if oc else CG // 2 * N4
                table = tables[oc, od][...]
                lhs = xb[:, :rows, : 2 * reach].reshape(GROUPS * rows, 2 * reach)
                result = jnp.dot(
                    lhs[:, :reach], table, preferred_element_type=jnp.float32
                ) + jnp.dot(lhs[:, reach:], table, preferred_element_type=jnp.float32)
                for pc in range(oc + 1):
                    for pd in range(od + 1):
                        column = (pc * (od + 1) + pd) * TILE
                        for k in range(GROUPS):
                            piece = result[k * rows : k * rows + rows, column : column + TILE]
                            if ob:
                                yb[2 * pc + pd, k, :N2] = piece
                                yb[2 * pc + pd, k, N2:] = piece[:QR]
                            else:
                                yb[2 * pc + pd, k, pl.ds(0, HB, stride=2)] = piece

    scale = weight[g]

    def add_up(wanted, blocks, target):
        for block in blocks:
            pb, pc, pd = BLOCKS[block]

            @pl.when(wanted & (pb <= fine_b) & (pc <= fine_c) & (pd <= fine_d))
            def _(block=block, pb=pb, part=2 * pc + pd):
                for h, sx, sy in SLOTS:
                    quarter = 2 * (sx ^ mine_x) + (sy ^ mine_y)
                    start = pl.multiple_of(quarter * 2 * QR, 2 * QR)
                    ref, index = target(block, h, sx, sy)
                    for j in range(GROUPS // 2):
                        k = h * (GROUPS // 2) + j
                        piece = yb[part, k, pl.ds(start, QR, stride=2)]
                        if pb:
                            piece = yb[part, k, pl.ds(start + 1, QR, stride=2)] - 0.5 * (
                                piece + yb[part, k, pl.ds(start + 2, QR, stride=2)]
                            )
                        where = index + (slice(None), slice(j * TILE, j * TILE + TILE))
                        ref[where] += scale * piece

    def slot_of(parts):
        return lambda block, h, sx, sy: (parts[h, sx, sy], (block, 0))

    def rest_of(ref):
        return lambda block, h, sx, sy: (ref, (h, sx, sy, block - SHARED_D, 0))

    def line_of(ref):
        return lambda block, h, sx, sy: (ref, (h, sx, sy, 0))

    if fine:
        add_up(active & even, range(SHARED_D), slot_of(e6))
        add_up(active & even, range(SHARED_D, SHARED_C), rest_of(e6_rest))
        add_up(active & odd, range(SHARED_D), slot_of(d6))
        add_up(active & odd, range(SHARED_D, SHARED_C), rest_of(d6_self))

        @pl.when((g == count - 1) & (i > 0))
        def _():
            for slot in SLOTS:
                d6[slot][...] -= 0.5 * e6[slot][...]
            d6_self[...] -= 0.5 * e6_rest[...]
    else:
        five = active & (level == 1)
        add_up(five, range(SHARED_D), slot_of(s5))
        add_up(five & (i < half_rows), range(SHARED_D, SHARED_C), rest_of(s5_low))
        add_up(five & (i >= half_rows), range(SHARED_D, SHARED_C), rest_of(s5_high))
        add_up(five, range(SHARED_C, 8), line_of(s5_self))
        add_up(active & (level == 0), range(1), line_of(s4))


def forward(fine, grids, scal, weight):
    count, rows_here = grids.shape[:2]
    half_rows = rows_here // 2
    tables = forward_tables()
    levels = scal[: 4 * count].reshape(count, 4)[:, 0]
    rows = scal[4 * count + 2] + jnp.arange(rows_here, dtype=jnp.int32)
    takes = (levels == 2) if fine else (levels < 2)
    takes = takes[None, :] & (rows[:, None] < (N1 // 4) * (1 << levels)[None, :])
    steps = jnp.arange(rows_here * count, dtype=jnp.int32)
    earlier = (steps[None, :] <= steps[:, None]) & takes.reshape(-1)[None, :]
    fetch = jnp.max(jnp.where(earlier, steps[None, :], 0), axis=1)

    def constant(table):
        return pl.BlockSpec(table.shape, lambda i, g, *_: (0, 0))

    def page(i, g, scal, fetch, weight):
        step = fetch[i * count + g]
        return (lax.rem(step, count), step // count, 0, 0)

    def rows_spec(blocks, row_of):
        return pl.BlockSpec(
            (blocks, 1, QR, HALF_LANES), lambda i, g, *_: (0, row_of(i), 0, 0)
        )

    def shape(*dims):
        return jax.ShapeDtypeStruct(dims + (QR, HALF_LANES), jnp.float32)

    def even_row(i):
        return i // 2

    def odd_row(i):
        return jnp.maximum(i - 1, 0) // 2

    rest = SHARED_C - SHARED_D
    if fine:
        out_specs = (
            [rows_spec(SHARED_D, even_row)] * 8
            + [rows_spec(SHARED_D, odd_row)] * 8
            + [rest_spec(rest, even_row), rest_spec(rest, odd_row)]
        )
        out_shape = [shape(SHARED_D, half_rows)] * 16 + [shape(2, 2, 2, rest, half_rows)] * 2
    else:
        out_specs = [rows_spec(SHARED_D, lambda i: i)] * 8 + [
            rest_spec(rest, lambda i: jnp.minimum(i, half_rows - 1)),
            rest_spec(rest, lambda i: jnp.maximum(i - half_rows, 0)),
            line_spec(lambda i: i),
            line_spec(lambda i: i),
        ]
        out_shape = (
            [shape(SHARED_D, rows_here)] * 8
            + [shape(2, 2, 2, rest, half_rows)] * 2
            + [shape(2, 2, 2, rows_here)] * 2
        )
    ordered = [tables[case] for case in CASES]
    return pl.pallas_call(
        lambda *refs: forward_kernel(fine, rows_here, count, *refs),
        grid_spec=pltpu.PrefetchScalarGridSpec(
            num_scalar_prefetch=3,
            grid=(rows_here, count),
            in_specs=[pl.BlockSpec((1, 1, N2, N3 * N4), page)]
            + [constant(table) for table in ordered],
            out_specs=out_specs,
            scratch_shapes=[
                pltpu.VMEM((GROUPS, 2 * HB, 2 * (CG + 2) * N4), jnp.bfloat16),
                pltpu.VMEM((4, GROUPS, N2 + QR, TILE), jnp.float32),
            ],
        ),
        out_shape=out_shape,
        compiler_params=pltpu.CompilerParams(vmem_limit_bytes=40 * 2**20),
        cost_estimate=pl.CostEstimate(
            flops=10**10, bytes_accessed=60 * 2**20, transcendentals=0
        ),
        name="split_fine" if fine else "split_coarse",
    )(scal, fetch, weight, grids, *ordered)


def rest_spec(blocks, row_of):
    return pl.BlockSpec(
        (2, 2, 2, blocks, 1, QR, HALF_LANES), lambda i, g, *_: (0, 0, 0, 0, row_of(i), 0, 0)
    )


def line_spec(row_of):
    return pl.BlockSpec(
        (2, 2, 2, 1, QR, HALF_LANES), lambda i, g, *_: (0, 0, 0, row_of(i), 0, 0)
    )


def backward_kernel(fine, rows_here, count, scal, order, *refs):
    used = 7 if fine else 20
    c6, c6_next, c6_rest, c6_rest_next, ahead_row, d6, d6_self = refs[:7]
    if not fine:
        c5 = dict(zip(SLOTS, refs[7:15]))
        c5_low, c5_high, s5_self = refs[15:18]
        c4 = refs[18]
    tables = dict(zip(CASES, refs[used : used + 4]))
    out = refs[used + 4]
    coarse, detail, joined, xb = refs[used + 5 :]
    half_rows = rows_here // 2
    i = pl.program_id(0)
    slot_number = pl.program_id(1)
    g = order[slot_number]
    level, fine_b, fine_c, fine_d = grid_facts(count, scal, g)
    mine_x = scal[4 * count]
    mine_y = scal[4 * count + 1]
    row = scal[4 * count + 2] + i
    odd = lax.rem(i, 2) == 1
    even = lax.rem(i, 2) == 0
    fresh = slot_number < order[count]
    inside = row < (N1 // 4) * (1 << level)
    active = fresh & inside

    def stage(wanted, blocks, source):
        for block in blocks:
            pb, pc, pd = BLOCKS[block]

            @pl.when(active & wanted & (pb <= fine_b) & (pc <= fine_c) & (pd <= fine_d))
            def _(block=block, work=(coarse, detail)[pb], part=2 * pc + pd):
                for h, sx, sy in SLOTS:
                    quarter = 2 * (sx ^ mine_x) + (sy ^ mine_y)
                    start = pl.multiple_of(quarter * QR, QR)
                    value = source(block, h, sx, sy)
                    for j in range(GROUPS // 2):
                        k = h * (GROUPS // 2) + j
                        work[part, k, pl.ds(start, QR)] = value[:, j * TILE : j * TILE + TILE]

    def here(block, h, sx, sy):
        if block < SHARED_D:
            return c6[h, sx, sy, block, 0]
        return c6_rest[h, sx, sy, block - SHARED_D, 0]

    def between(last):
        def value(block, h, sx, sy):
            if last:
                after = ahead_row[h, sx, sy, block, 0]
            elif block < SHARED_D:
                after = c6_next[h, sx, sy, block, 0]
            else:
                after = c6_rest_next[h, sx, sy, block - SHARED_D, 0]
            mean = 0.5 * (here(block, h, sx, sy) + after)
            if block < SHARED_D:
                return mean + d6[h, sx, sy, block, 0]
            return mean + d6_self[h, sx, sy, block - SHARED_D, 0]

        return value

    stage((level == 2) & even, range(SHARED_C), here)
    if half_rows > 1:
        stage((level == 2) & odd & (i < rows_here - 1), range(SHARED_C), between(False))
    stage((level == 2) & odd & (i == rows_here - 1), range(SHARED_C), between(True))
    if not fine:
        rest = range(SHARED_D, SHARED_C)
        five = level == 1
        stage(five, range(SHARED_D), lambda b, h, x, y: c5[h, x, y][b, 0])
        stage(five & (i < half_rows), rest, lambda b, h, x, y: c5_low[h, x, y, b - SHARED_D, 0])
        stage(five & (i >= half_rows), rest, lambda b, h, x, y: c5_high[h, x, y, b - SHARED_D, 0])
        stage(five, range(SHARED_C, 8), lambda b, h, x, y: s5_self[h, x, y, 0])
        stage(level == 0, range(1), lambda b, h, x, y: c4[h, x, y, 0])

    @pl.when(fresh & jnp.logical_not(inside))
    def _():
        out[...] = jnp.zeros_like(out)

    for oc, od in CASES:
        for ob in range(2):
            @pl.when(active & (fine_b == ob) & (fine_c == oc) & (fine_d == od))
            def _(oc=oc, od=od, ob=ob):
                parts = [(pc, pd) for pc in range(oc + 1) for pd in range(od + 1)]
                ahead = [(0, pd) for pd in range(od + 1)] if oc else []
                reach = (len(parts) + len(ahead)) * TILE
                rows = (1 + ob) * HB
                for place, (pc, pd) in enumerate(parts):
                    part = 2 * pc + pd
                    for k in range(GROUPS):
                        value = coarse[part, k, :HB]
                        if ob:
                            coarse[part, k, HB:] = coarse[part, k, :QR]
                            mean = 0.5 * (value + coarse[part, k, 1 : HB + 1])
                            joined[k, pl.ds(0, HB, stride=2)] = value
                            joined[k, pl.ds(1, HB, stride=2)] = detail[part, k] + mean
                            value = joined[k]
                        for base, piece in zip((0, reach), split_parts(value)):
                            start = base + place * TILE
                            xb[k, :rows, start : start + TILE] = piece
                            if oc and not pc:
                                start = base + (len(parts) + pd) * TILE
                                before = (k + GROUPS - 1) % GROUPS
                                xb[before, :rows, start : start + TILE] = piece
                table = tables[oc, od][...]
                lhs = xb[:, :rows, : 2 * reach].reshape(GROUPS * rows, 2 * reach)
                result = jnp.dot(
                    lhs[:, :reach], table, preferred_element_type=jnp.float32
                ) + jnp.dot(lhs[:, reach:], table, preferred_element_type=jnp.float32)
                span = CG * N4 if oc else CG // 2 * N4
                for k in range(GROUPS):
                    out[0, 0, :rows, k * span : k * span + span] = result[
                        k * rows : k * rows + rows
                    ]
                if not ob:
                    out[0, 0, HB:, :] = jnp.zeros((HB, N3 * N4), jnp.float32)
                if not oc:
                    out[0, 0, :, HC * N4 :] = jnp.zeros((N2, HC * N4), jnp.float32)


def backward(fine, count, scal, rows_here, values, before=None):
    half_rows = rows_here // 2
    tables = backward_tables()
    ordered = [tables[case] for case in CASES]
    levels = scal[: 4 * count].reshape(count, 4)[:, 0]
    takes = (levels == 2) if fine else (levels < 2)
    number = jnp.maximum(jnp.sum(takes.astype(jnp.int32)), 1)
    spots = jnp.arange(count, dtype=jnp.int32)
    before_me = (spots[None, :] < spots[:, None]).astype(jnp.int32)
    takes_int = takes.astype(jnp.int32)
    rank = jnp.where(
        takes,
        jnp.sum(before_me * takes_int[None, :], axis=1),
        jnp.sum(takes_int) + jnp.sum(before_me * (1 - takes_int)[None, :], axis=1),
    )
    wanted = jnp.minimum(spots, number - 1)
    order = jnp.sum(jnp.where(rank[None, :] == wanted[:, None], spots[None, :], 0), axis=1)
    order = jnp.concatenate([order, number[None]]).astype(jnp.int32)

    def constant(table):
        return pl.BlockSpec(table.shape, lambda i, g, *_: (0, 0))

    def page(i, g, scal, order):
        return (order[g], i, 0, 0)

    rest = SHARED_C - SHARED_D
    c6, c6_rest, ahead_row, d6, d6_self = values[:5]
    operands = [c6, c6, c6_rest, c6_rest, ahead_row, d6, d6_self]
    following = lambda i: jnp.minimum((i + 1) // 2, half_rows - 1)
    in_specs = [
        rest_spec(SHARED_D, lambda i: i // 2),
        rest_spec(SHARED_D, following),
        rest_spec(rest, lambda i: i // 2),
        rest_spec(rest, following),
        rest_spec(SHARED_C, lambda i: 0),
        rest_spec(SHARED_D, lambda i: i // 2),
        rest_spec(rest, lambda i: i // 2),
    ]
    aliases = {}
    if not fine:
        c5, c5_low, c5_high, s5_self = values[5:]
        operands += [c5[slot] for slot in SLOTS] + [c5_low, c5_high, s5_self]
        in_specs += [
            pl.BlockSpec((SHARED_D, 1, QR, HALF_LANES), lambda i, g, *_: (0, i, 0, 0))
        ] * 8 + [
            rest_spec(rest, lambda i: jnp.minimum(i, half_rows - 1)),
            rest_spec(rest, lambda i: jnp.maximum(i - half_rows, 0)),
            line_spec(lambda i: i),
        ]
        c4 = jnp.stack([c5[slot][SHARED_D] for slot in SLOTS])
        operands += [c4.reshape((2, 2, 2) + c4.shape[1:]), before]
        in_specs += [line_spec(lambda i: i), pl.BlockSpec(memory_space=pl.ANY)]
        aliases = {2 + len(operands) - 1: 0}
    return pl.pallas_call(
        lambda *refs: backward_kernel(fine, rows_here, count, *refs),
        grid_spec=pltpu.PrefetchScalarGridSpec(
            num_scalar_prefetch=2,
            grid=(rows_here, count),
            in_specs=in_specs + [constant(table) for table in ordered],
            out_specs=pl.BlockSpec((1, 1, N2, N3 * N4), page),
            scratch_shapes=[
                pltpu.VMEM((4, GROUPS, HB + QR, TILE), jnp.float32),
                pltpu.VMEM((4, GROUPS, HB, TILE), jnp.float32),
                pltpu.VMEM((GROUPS, N2, TILE), jnp.float32),
                pltpu.VMEM((GROUPS, N2, 12 * TILE), jnp.bfloat16),
            ],
        ),
        out_shape=jax.ShapeDtypeStruct((count, rows_here, N2, N3 * N4), jnp.float32),
        input_output_aliases=aliases,
        compiler_params=pltpu.CompilerParams(vmem_limit_bytes=40 * 2**20),
        cost_estimate=pl.CostEstimate(
            flops=10**10, bytes_accessed=60 * 2**20, transcendentals=0
        ),
        name="join_fine" if fine else "join_coarse",
    )(scal, order, *operands, *ordered)


def stack_slots(pieces):
    return jnp.stack(
        [
            jnp.stack([jnp.stack([pieces[h, sx, sy] for sy in range(2)]) for sx in range(2)])
            for h in range(2)
        ]
    )


def exchange(value, axis, domains):
    dom_count = lax.axis_size("dom")
    pairs = []
    for x in range(2):
        for y in range(2):
            other = (1 - x, y) if axis == "half" else (x, 1 - y)
            for d in range(domains):
                pairs.append(
                    ((x * 2 + y) * dom_count + d, (other[0] * 2 + other[1]) * dom_count + d)
                )
    return lax.ppermute(value, ("half", "grid", "dom"), pairs)


def reduce_quarter(pieces, domains):
    reduced = []
    for h in range(2):
        first, second = (("half", "grid"), ("grid", "half"))[h]
        far = lambda a, b: pieces[(h, a, b) if h == 0 else (h, b, a)]
        onward = far(0, 1) + exchange(far(1, 1), first, domains)
        nearby = far(0, 0) + exchange(far(1, 0), first, domains)
        reduced.append(nearby + exchange(onward, second, domains))
    return jnp.stack(reduced)


def gather_quarters(own, domains):
    pieces = {}
    for h in range(2):
        first, second = (("half", "grid"), ("grid", "half"))[h]
        place = lambda a, b: (h, a, b) if h == 0 else (h, b, a)
        pieces[place(0, 0)] = own[h]
        pieces[place(0, 1)] = exchange(own[h], second, domains)
        pieces[place(1, 0)] = exchange(own[h], first, domains)
        pieces[place(1, 1)] = exchange(pieces[place(0, 1)], first, domains)
    return pieces


def rows_up(value, sources):
    half_rows = value.shape[-3] // 2
    low = lax.ppermute(value[..., :half_rows, :, :], "dom", [(d, 2 * d) for d in range(sources)])
    high = lax.ppermute(
        value[..., half_rows:, :, :], "dom", [(d, 2 * d + 1) for d in range(sources)]
    )
    return low + high


def rows_down(value):
    targets = lax.axis_size("dom") // 2
    low = lax.ppermute(value, "dom", [(2 * d, d) for d in range(targets)])
    high = lax.ppermute(value, "dom", [(2 * d + 1, d) for d in range(targets)])
    return jnp.concatenate([low, high], axis=-3)


def next_row(value, devices):
    return lax.ppermute(
        value[..., :1, :, :], "dom", [((d + 1) % devices, d) for d in range(devices)]
    )


def per_device(grids, levels):
    count, rows_here = grids.shape[:2]
    half_rows = rows_here // 2
    half_size = lax.axis_size("half")
    grid_size = lax.axis_size("grid")
    dom_size = lax.axis_size("dom")
    square = half_size == 2 and grid_size == 2
    group = lax.axis_index("half") * grid_size + lax.axis_index("grid")
    weights = combination_weights(levels).astype(jnp.float32)
    lowest = jnp.array(
        [LEV1 - SPANS[0], LEV2 - SPANS[1], LEV3 - SPANS[2], LEV4 - SPANS[3]], dtype=jnp.int32
    )
    offsets = levels - lowest[None, :]
    own_offsets = lax.dynamic_slice_in_dim(offsets, group * count, count, 0)
    own_weights = lax.dynamic_slice_in_dim(weights, group * count, count, 0)
    zero = jnp.zeros((), jnp.int32)
    place = jnp.stack(
        [
            lax.axis_index("half") if square else zero,
            lax.axis_index("grid") if square else zero,
            lax.axis_index("dom") * rows_here,
        ]
    ).astype(jnp.int32)
    scal = jnp.concatenate([own_offsets.reshape(-1), place])
    coarse_parts = forward(False, grids, scal, own_weights)
    s5 = dict(zip(SLOTS, coarse_parts[:8]))
    s5_low, s5_high, s5_self, s4 = coarse_parts[8:]
    fine_parts = forward(True, grids, scal, own_weights)
    e6 = dict(zip(SLOTS, fine_parts[:8]))
    d6 = dict(zip(SLOTS, fine_parts[8:16]))
    e6_rest, d6_self = fine_parts[16:]
    sources = dom_size // 2
    quarter_devices = dom_size // 4

    c6_rest = (
        e6_rest
        + lax.ppermute(s5_low, "dom", [(d, 2 * d) for d in range(sources)])
        + lax.ppermute(s5_high, "dom", [(d, 2 * d + 1) for d in range(sources)])
    )
    firsts = jnp.concatenate(
        [stack_slots({slot: e6[slot][:, :1] for slot in SLOTS}), e6_rest[..., :1, :, :]], axis=3
    )
    e6_ahead = next_row(firsts, dom_size)
    d6_self = d6_self.at[..., -1:, :, :].add(-0.5 * e6_ahead[:, :, :, SHARED_D:])
    d6 = {
        slot: d6[slot].at[:, -1:].add(-0.5 * e6_ahead[slot][:SHARED_D]) for slot in SLOTS
    }

    s4 = s4[:, :, :, None]
    ahead = next_row(s4, quarter_devices)
    longer = jnp.concatenate([s4, ahead], axis=-3)
    mids = 0.5 * (longer[..., :-1, :, :] + longer[..., 1:, :, :])
    spread = jnp.stack([s4, mids], axis=-3).reshape(
        s4.shape[:-3] + (2 * rows_here,) + s4.shape[-2:]
    )
    coarsest = rows_up(rows_up(spread, quarter_devices), sources)
    e6 = {slot: e6[slot].at[:1].add(coarsest[slot]) for slot in SLOTS}

    if square:
        s5_own = reduce_quarter(s5, sources)
        d6_own = reduce_quarter(d6, dom_size)
        e6_own = reduce_quarter(e6, dom_size)
        rest_own = reduce_quarter({slot: c6_rest[slot] for slot in SLOTS}, dom_size)
    else:
        s5_own, e6_own, d6_own, rest_own = lax.psum(
            (stack_slots(s5), stack_slots(e6), stack_slots(d6), c6_rest), ("half", "grid")
        )
    c6_own = e6_own + rows_up(s5_own, sources)
    c5_own = rows_down(c6_own)
    c4_own = rows_down(c5_own[..., :1, ::2, :, :])
    c5_own = jnp.concatenate([c5_own, c4_own], axis=-4)
    ahead_own = next_row(
        jnp.concatenate([c6_own[..., :1, :, :], rest_own[..., :1, :, :]], axis=-4), dom_size
    )
    if square:
        d6 = stack_slots(gather_quarters(d6_own, dom_size))
        c6_rest = stack_slots(gather_quarters(rest_own, dom_size))
        c6 = stack_slots(gather_quarters(c6_own, dom_size))
        ahead_row = stack_slots(gather_quarters(ahead_own, dom_size))
        c5 = gather_quarters(c5_own, sources)
    else:
        c6, d6, c6_rest, ahead_row = c6_own, d6_own, rest_own, ahead_own
        c5 = {slot: c5_own[slot] for slot in SLOTS}
    c5_low = lax.ppermute(c6_rest, "dom", [(2 * d, d) for d in range(sources)])
    c5_high = lax.ppermute(c6_rest, "dom", [(2 * d + 1, d) for d in range(sources)])
    values = [c6, c6_rest, ahead_row, d6, d6_self]
    written = backward(True, count, scal, rows_here, values)
    values += [c5, c5_low, c5_high, s5_self]
    return backward(False, count, scal, rows_here, values, written)


def solution(mesh):
    return jax.shard_map(
        per_device,
        mesh=mesh,
        in_specs=(P(("half", "grid"), "dom", None, None), P()),
        out_specs=P(("half", "grid"), "dom", None, None),
        check_vma=False,
    )
```

```python
import jax
import jax.numpy as jnp
import numpy as np
from jax import lax
from jax.experimental import pallas as pl
from jax.experimental.pallas import tpu as pltpu
from jax.sharding import PartitionSpec as P


LEV1 = 6
LEV2 = 6
LEV3 = 6
LEV4 = 6
N1 = 64
N2 = 64
N3 = 64
N4 = 64
SPANS = (2, 1, 1, 1)


BLOCKS = (
    (0, 0, 0), (1, 0, 0), (0, 1, 0), (0, 0, 1),
    (1, 1, 0), (1, 0, 1), (0, 1, 1), (1, 1, 1),
)
SHARED_D = 4
SHARED_C = 7
HB = N2 // 2
HC = N3 // 2
HD = N4 // 2
GROUPS = 8
CG = N3 // GROUPS
LANES = HC * HD
HALF_LANES = LANES // 2
QR = HB // 4
TILE = CG // 2 * HD
SLOTS = tuple((h, sx, sy) for h in range(2) for sx in range(2) for sy in range(2))


def combination_weights(levels):
    corners = np.array(
        [[corner >> place & 1 for place in range(4)] for corner in range(16)], dtype=np.int32
    )
    parity = 1 - 2 * (corners.sum(axis=1) % 2)
    raised = levels[:, None, :] + jnp.asarray(corners, dtype=jnp.int32)[None, :, :]
    below = jnp.all(raised[:, :, None, :] <= levels[None, None, :, :], axis=3)
    inside = jnp.any(below, axis=2).astype(jnp.int32)
    return jnp.sum(inside * jnp.asarray(parity, dtype=jnp.int32)[None, :], axis=1)


def split_matrix(count_in, half, wrap):
    table = np.zeros((count_in, 2, half))
    for k in range(half):
        table[2 * k, 0, k] = 1.0
        table[2 * k + 1, 1, k] += 1.0
        table[2 * k, 1, k] -= 0.5
        table[(2 * k + 2) % wrap, 1, k] -= 0.5
    return table


def plain_matrix(count_in, half):
    table = np.zeros((count_in, 1, half))
    for k in range(half):
        table[k, 0, k] = 1.0
    return table


def join_matrix(parts_in, half_out, wrap, next_points):
    table = np.zeros((parts_in, half_out + next_points, 2 * half_out))
    for k in range(half_out):
        table[0, k, 2 * k] = 1.0
        table[1, k, 2 * k + 1] += 1.0
        table[0, k, 2 * k + 1] += 0.5
        table[0, (k + 1) % wrap, 2 * k + 1] += 0.5
    return table


def forward_tables():
    half_c = CG // 2
    tables = {}
    for oc in range(2):
        for od in range(2):
            if oc:
                along_c = split_matrix(CG + 2, half_c, CG + 2)
            else:
                along_c = plain_matrix(half_c, half_c)
            along_d = split_matrix(N4, HD, N4) if od else plain_matrix(N4, HD)
            table = np.einsum("cpk,dql->cdpqkl", along_c, along_d)
            rows = along_c.shape[0] * N4
            tables[oc, od] = jnp.asarray(table.reshape(rows, -1), jnp.bfloat16)
    return tables


def backward_tables():
    half_c = CG // 2
    tables = {}
    for oc in range(2):
        for od in range(2):
            if od:
                along_d = join_matrix(2, HD, HD, 0)
            else:
                along_d = np.zeros((1, HD, N4))
                along_d[0, np.arange(HD), np.arange(HD)] = 1.0
            if oc:
                along_c = join_matrix(2, half_c, half_c + half_c, half_c)
                own = np.einsum("pkc,qld->pqklcd", along_c[:, :half_c], along_d)
                ahead = np.einsum("pkc,qld->pqklcd", along_c[:1, half_c:], along_d)
                cols = CG * N4
                table = np.concatenate([own.reshape(-1, cols), ahead.reshape(-1, cols)], axis=0)
            else:
                along_c = np.eye(half_c)[None]
                table = np.einsum("pkc,qld->pqklcd", along_c, along_d).reshape(-1, half_c * N4)
            tables[oc, od] = jnp.asarray(table, jnp.bfloat16)
    return tables


CASES = ((0, 0), (0, 1), (1, 0), (1, 1))


def split_parts(value):
    high = value.astype(jnp.bfloat16)
    low = (value - high.astype(jnp.float32)).astype(jnp.bfloat16)
    return high, low


def grid_facts(scal, g):
    return tuple(scal[4 * g + axis] for axis in range(4))


def forward_kernel(fine, rows_here, count, scal, fetch, weight, x_ref, *refs):
    tables = dict(zip(CASES, refs[:4]))
    outs = refs[4:-2]
    xb, yb = refs[-2:]
    half_rows = rows_here // 2
    i = pl.program_id(0)
    g = pl.program_id(1)
    level, fine_b, fine_c, fine_d = grid_facts(scal, g)
    mine_x = scal[4 * count]
    mine_y = scal[4 * count + 1]
    row = scal[4 * count + 2] + i
    odd = lax.rem(i, 2) == 1
    even = lax.rem(i, 2) == 0
    active = row < (N1 // 4) * (1 << level)
    active = active & (level == (2 if fine else 1))

    def clear(wanted, *targets):
        @pl.when((g == 0) & wanted)
        def _():
            for target in targets:
                target[...] = jnp.zeros_like(target)

    if fine:
        e6 = dict(zip(SLOTS, outs[:8]))
        d6 = dict(zip(SLOTS, outs[8:16]))
        e6_rest, d6_self = outs[16:]
        clear(even, *outs[:8], e6_rest)
        clear(odd, *outs[8:16], d6_self)
    else:
        s5 = dict(zip(SLOTS, outs[:8]))
        s5_low, s5_high, s5_self = outs[8:]
        clear(i >= 0, *outs[:8], s5_self)
        clear(i < half_rows, s5_low)
        clear(i >= half_rows, s5_high)

    def put(values, fine_c_here):
        rows = slice(0, values.shape[0])
        high, low = split_parts(values)
        span = CG * N4 if fine_c_here else CG // 2 * N4
        reach = span + 2 * N4 if fine_c_here else span
        for k in range(GROUPS):
            for place, piece in ((0, high), (reach, low)):
                xb[k, rows, place : place + span] = piece[:, k * span : k * span + span]
                if fine_c_here:
                    ahead = (k + 1) % GROUPS * span
                    xb[k, rows, place + span : place + reach] = piece[:, ahead : ahead + 2 * N4]

    for oc, od in CASES:
        for ob in range(2):
            @pl.when(active & (fine_b == ob) & (fine_c == oc) & (fine_d == od))
            def _(oc=oc, od=od, ob=ob):
                lanes = N3 * N4 if oc else HC * N4
                rows = (1 + ob) * HB
                put(x_ref[0, 0, :rows, :lanes], oc)
                reach = (CG + 2) * N4 if oc else CG // 2 * N4
                table = tables[oc, od][...]
                lhs = xb[:, :rows, : 2 * reach].reshape(GROUPS * rows, 2 * reach)
                result = jnp.dot(
                    lhs[:, :reach], table, preferred_element_type=jnp.float32
                ) + jnp.dot(lhs[:, reach:], table, preferred_element_type=jnp.float32)
                for pc in range(oc + 1):
                    for pd in range(od + 1):
                        column = (pc * (od + 1) + pd) * TILE
                        for k in range(GROUPS):
                            piece = result[k * rows : k * rows + rows, column : column + TILE]
                            if ob:
                                yb[2 * pc + pd, k, :N2] = piece
                                yb[2 * pc + pd, k, N2:] = piece[:QR]
                            else:
                                yb[2 * pc + pd, k, pl.ds(0, HB, stride=2)] = piece

    scale = weight[g]

    def add_up(wanted, blocks, target):
        for block in blocks:
            pb, pc, pd = BLOCKS[block]

            @pl.when(wanted & (pb <= fine_b) & (pc <= fine_c) & (pd <= fine_d))
            def _(block=block, pb=pb, part=2 * pc + pd):
                for h, sx, sy in SLOTS:
                    quarter = 2 * (sx ^ mine_x) + (sy ^ mine_y)
                    start = pl.multiple_of(quarter * 2 * QR, 2 * QR)
                    ref, index = target(block, h, sx, sy)
                    for j in range(GROUPS // 2):
                        k = h * (GROUPS // 2) + j
                        piece = yb[part, k, pl.ds(start, QR, stride=2)]
                        if pb:
                            piece = yb[part, k, pl.ds(start + 1, QR, stride=2)] - 0.5 * (
                                piece + yb[part, k, pl.ds(start + 2, QR, stride=2)]
                            )
                        where = index + (slice(None), slice(j * TILE, j * TILE + TILE))
                        ref[where] += scale * piece

    def slot_of(parts):
        return lambda block, h, sx, sy: (parts[h, sx, sy], (block, 0))

    def rest_of(ref):
        return lambda block, h, sx, sy: (ref, (h, sx, sy, block - SHARED_D, 0))

    def line_of(ref):
        return lambda block, h, sx, sy: (ref, (h, sx, sy, 0))

    if fine:
        add_up(active & even, range(SHARED_D), slot_of(e6))
        add_up(active & even, range(SHARED_D, SHARED_C), rest_of(e6_rest))
        add_up(active & odd, range(SHARED_D), slot_of(d6))
        add_up(active & odd, range(SHARED_D, SHARED_C), rest_of(d6_self))

        @pl.when((g == count - 1) & (i > 0))
        def _():
            for slot in SLOTS:
                d6[slot][...] -= 0.5 * e6[slot][...]
            d6_self[...] -= 0.5 * e6_rest[...]
    else:
        five = active
        add_up(five, range(SHARED_D), slot_of(s5))
        add_up(five & (i < half_rows), range(SHARED_D, SHARED_C), rest_of(s5_low))
        add_up(five & (i >= half_rows), range(SHARED_D, SHARED_C), rest_of(s5_high))
        add_up(five, range(SHARED_C, 8), line_of(s5_self))


def forward(fine, grids, scal, weight):
    count, rows_here = grids.shape[:2]
    half_rows = rows_here // 2
    tables = forward_tables()
    levels = scal[: 4 * count].reshape(count, 4)[:, 0]
    rows = scal[4 * count + 2] + jnp.arange(rows_here, dtype=jnp.int32)
    takes = levels == (2 if fine else 1)
    takes = takes[None, :] & (rows[:, None] < (N1 // 4) * (1 << levels)[None, :])
    steps = jnp.arange(rows_here * count, dtype=jnp.int32)
    earlier = (steps[None, :] <= steps[:, None]) & takes.reshape(-1)[None, :]
    fetch = jnp.max(jnp.where(earlier, steps[None, :], 0), axis=1)

    def constant(table):
        return pl.BlockSpec(table.shape, lambda i, g, *_: (0, 0))

    def page(i, g, scal, fetch, weight):
        step = fetch[i * count + g]
        return (lax.rem(step, count), step // count, 0, 0)

    def rows_spec(blocks, row_of):
        return pl.BlockSpec(
            (blocks, 1, QR, HALF_LANES), lambda i, g, *_: (0, row_of(i), 0, 0)
        )

    def shape(*dims):
        return jax.ShapeDtypeStruct(dims + (QR, HALF_LANES), jnp.float32)

    def even_row(i):
        return i // 2

    def odd_row(i):
        return jnp.maximum(i - 1, 0) // 2

    rest = SHARED_C - SHARED_D
    if fine:
        out_specs = (
            [rows_spec(SHARED_D, even_row)] * 8
            + [rows_spec(SHARED_D, odd_row)] * 8
            + [rest_spec(rest, even_row), rest_spec(rest, odd_row)]
        )
        out_shape = [shape(SHARED_D, half_rows)] * 16 + [shape(2, 2, 2, rest, half_rows)] * 2
    else:
        out_specs = [rows_spec(SHARED_D, lambda i: i)] * 8 + [
            rest_spec(rest, lambda i: jnp.minimum(i, half_rows - 1)),
            rest_spec(rest, lambda i: jnp.maximum(i - half_rows, 0)),
            line_spec(lambda i: i),
        ]
        out_shape = (
            [shape(SHARED_D, rows_here)] * 8
            + [shape(2, 2, 2, rest, half_rows)] * 2
            + [shape(2, 2, 2, rows_here)]
        )
    ordered = [tables[case] for case in CASES]
    return pl.pallas_call(
        lambda *refs: forward_kernel(fine, rows_here, count, *refs),
        grid_spec=pltpu.PrefetchScalarGridSpec(
            num_scalar_prefetch=3,
            grid=(rows_here, count),
            in_specs=[pl.BlockSpec((1, 1, N2, N3 * N4), page)]
            + [constant(table) for table in ordered],
            out_specs=out_specs,
            scratch_shapes=[
                pltpu.VMEM((GROUPS, 2 * HB, 2 * (CG + 2) * N4), jnp.bfloat16),
                pltpu.VMEM((4, GROUPS, N2 + QR, TILE), jnp.float32),
            ],
        ),
        out_shape=out_shape,
        compiler_params=pltpu.CompilerParams(vmem_limit_bytes=60 * 2**20),
        cost_estimate=pl.CostEstimate(
            flops=10**10, bytes_accessed=60 * 2**20, transcendentals=0
        ),
        name="split_fine" if fine else "split_coarse",
    )(scal, fetch, weight, grids, *ordered)


def coarsest_kernel(count, scal, weight, x_ref, table, out, yb):
    i = pl.program_id(0)
    g = pl.program_id(1)
    mine_x = scal[4 * count]
    mine_y = scal[4 * count + 1]
    active = (scal[4 * g] == 0) & (scal[4 * count + 2] + i < N1 // 4)

    @pl.when(g == 0)
    def _():
        out[...] = jnp.zeros_like(out)

    @pl.when(active)
    def _():
        span = CG // 2 * N4
        for k in range(GROUPS):
            high, low = split_parts(x_ref[0, 0, :, k * span : k * span + span])
            yb[k] = weight[g] * (
                jnp.dot(high, table[...], preferred_element_type=jnp.float32)
                + jnp.dot(low, table[...], preferred_element_type=jnp.float32)
            )
        for h, sx, sy in SLOTS:
            quarter = 2 * (sx ^ mine_x) + (sy ^ mine_y)
            start = pl.multiple_of(quarter * QR, QR)
            for j in range(GROUPS // 2):
                out[h, sx, sy, 0, :, j * TILE : j * TILE + TILE] += yb[
                    h * (GROUPS // 2) + j, pl.ds(start, QR)
                ]


def coarsest(grids, scal, weight):
    count, rows_here = grids.shape[:2]
    table = forward_tables()[0, 0]

    def page(i, g, scal, weight):
        wanted = (scal[4 * g] == 0) & (scal[4 * count + 2] + i < N1 // 4)
        return (jnp.where(wanted, g, 0), jnp.where(wanted, i, 0), 0, 0)

    return pl.pallas_call(
        lambda *refs: coarsest_kernel(count, *refs),
        grid_spec=pltpu.PrefetchScalarGridSpec(
            num_scalar_prefetch=2,
            grid=(rows_here, count),
            in_specs=[
                pl.BlockSpec((1, 1, HB, HC * N4), page),
                pl.BlockSpec(table.shape, lambda i, g, *_: (0, 0)),
            ],
            out_specs=line_spec(lambda i: i),
            scratch_shapes=[pltpu.VMEM((GROUPS, HB, TILE), jnp.float32)],
        ),
        out_shape=jax.ShapeDtypeStruct((2, 2, 2, rows_here, QR, HALF_LANES), jnp.float32),
        compiler_params=pltpu.CompilerParams(vmem_limit_bytes=60 * 2**20),
        cost_estimate=pl.CostEstimate(
            flops=10**8, bytes_accessed=4 * 2**20, transcendentals=0
        ),
        name="split_coarsest",
    )(scal, weight, grids, table)


def rest_spec(blocks, row_of):
    return pl.BlockSpec(
        (2, 2, 2, blocks, 1, QR, HALF_LANES), lambda i, g, *_: (0, 0, 0, 0, row_of(i), 0, 0)
    )


def line_spec(row_of):
    return pl.BlockSpec(
        (2, 2, 2, 1, QR, HALF_LANES), lambda i, g, *_: (0, 0, 0, row_of(i), 0, 0)
    )


def backward_kernel(fine, rows_here, count, scal, order, *refs):
    used = 7 if fine else 20
    c6, c6_next, c6_rest, c6_rest_next, ahead_row, d6, d6_self = refs[:7]
    if not fine:
        c5 = dict(zip(SLOTS, refs[7:15]))
        c5_low, c5_high, s5_self = refs[15:18]
        c4 = refs[18]
    tables = dict(zip(CASES, refs[used : used + 4]))
    out = refs[used + 4]
    coarse, detail, joined, xb = refs[used + 5 :]
    half_rows = rows_here // 2
    i = pl.program_id(0)
    slot_number = pl.program_id(1)
    g = order[slot_number]
    level, fine_b, fine_c, fine_d = grid_facts(scal, g)
    mine_x = scal[4 * count]
    mine_y = scal[4 * count + 1]
    row = scal[4 * count + 2] + i
    odd = lax.rem(i, 2) == 1
    even = lax.rem(i, 2) == 0
    fresh = slot_number < order[count]
    inside = row < (N1 // 4) * (1 << level)
    active = fresh & inside

    def stage(wanted, blocks, source):
        for block in blocks:
            pb, pc, pd = BLOCKS[block]

            @pl.when(active & wanted & (pb <= fine_b) & (pc <= fine_c) & (pd <= fine_d))
            def _(block=block, work=(coarse, detail)[pb], part=2 * pc + pd):
                for h, sx, sy in SLOTS:
                    quarter = 2 * (sx ^ mine_x) + (sy ^ mine_y)
                    start = pl.multiple_of(quarter * QR, QR)
                    value = source(block, h, sx, sy)
                    for j in range(GROUPS // 2):
                        k = h * (GROUPS // 2) + j
                        work[part, k, pl.ds(start, QR)] = value[:, j * TILE : j * TILE + TILE]

    def here(block, h, sx, sy):
        if block < SHARED_D:
            return c6[h, sx, sy, block, 0]
        return c6_rest[h, sx, sy, block - SHARED_D, 0]

    def between(last):
        def value(block, h, sx, sy):
            if last:
                after = ahead_row[h, sx, sy, block, 0]
            elif block < SHARED_D:
                after = c6_next[h, sx, sy, block, 0]
            else:
                after = c6_rest_next[h, sx, sy, block - SHARED_D, 0]
            mean = 0.5 * (here(block, h, sx, sy) + after)
            if block < SHARED_D:
                return mean + d6[h, sx, sy, block, 0]
            return mean + d6_self[h, sx, sy, block - SHARED_D, 0]

        return value

    stage((level == 2) & even, range(SHARED_C), here)
    if half_rows > 1:
        stage((level == 2) & odd & (i < rows_here - 1), range(SHARED_C), between(False))
    stage((level == 2) & odd & (i == rows_here - 1), range(SHARED_C), between(True))
    if not fine:
        rest = range(SHARED_D, SHARED_C)
        five = level == 1
        stage(five, range(SHARED_D), lambda b, h, x, y: c5[h, x, y][b, 0])
        stage(five & (i < half_rows), rest, lambda b, h, x, y: c5_low[h, x, y, b - SHARED_D, 0])
        stage(five & (i >= half_rows), rest, lambda b, h, x, y: c5_high[h, x, y, b - SHARED_D, 0])
        stage(five, range(SHARED_C, 8), lambda b, h, x, y: s5_self[h, x, y, 0])
        stage(level == 0, range(1), lambda b, h, x, y: c4[h, x, y, 0])

    @pl.when(fresh & jnp.logical_not(inside))
    def _():
        out[...] = jnp.zeros_like(out)

    for oc, od in CASES:
        for ob in range(2):
            @pl.when(active & (fine_b == ob) & (fine_c == oc) & (fine_d == od))
            def _(oc=oc, od=od, ob=ob):
                parts = [(pc, pd) for pc in range(oc + 1) for pd in range(od + 1)]
                ahead = [(0, pd) for pd in range(od + 1)] if oc else []
                reach = (len(parts) + len(ahead)) * TILE
                rows = (1 + ob) * HB
                for place, (pc, pd) in enumerate(parts):
                    part = 2 * pc + pd
                    for k in range(GROUPS):
                        value = coarse[part, k, :HB]
                        if ob:
                            coarse[part, k, HB:] = coarse[part, k, :QR]
                            mean = 0.5 * (value + coarse[part, k, 1 : HB + 1])
                            joined[k, pl.ds(0, HB, stride=2)] = value
                            joined[k, pl.ds(1, HB, stride=2)] = detail[part, k] + mean
                            value = joined[k]
                        for base, piece in zip((0, reach), split_parts(value)):
                            start = base + place * TILE
                            xb[k, :rows, start : start + TILE] = piece
                            if oc and not pc:
                                start = base + (len(parts) + pd) * TILE
                                before = (k + GROUPS - 1) % GROUPS
                                xb[before, :rows, start : start + TILE] = piece
                table = tables[oc, od][...]
                lhs = xb[:, :rows, : 2 * reach].reshape(GROUPS * rows, 2 * reach)
                result = jnp.dot(
                    lhs[:, :reach], table, preferred_element_type=jnp.float32
                ) + jnp.dot(lhs[:, reach:], table, preferred_element_type=jnp.float32)
                span = CG * N4 if oc else CG // 2 * N4
                for k in range(GROUPS):
                    out[0, 0, :rows, k * span : k * span + span] = result[
                        k * rows : k * rows + rows
                    ]
                if not ob:
                    out[0, 0, HB:, :] = jnp.zeros((HB, N3 * N4), jnp.float32)
                if not oc:
                    out[0, 0, :, HC * N4 :] = jnp.zeros((N2, HC * N4), jnp.float32)


def backward(fine, count, scal, rows_here, values, before=None):
    half_rows = rows_here // 2
    tables = backward_tables()
    ordered = [tables[case] for case in CASES]
    levels = scal[: 4 * count].reshape(count, 4)[:, 0]
    takes = (levels == 2) if fine else (levels < 2)
    number = jnp.maximum(jnp.sum(takes.astype(jnp.int32)), 1)
    spots = jnp.arange(count, dtype=jnp.int32)
    before_me = (spots[None, :] < spots[:, None]).astype(jnp.int32)
    takes_int = takes.astype(jnp.int32)
    rank = jnp.where(
        takes,
        jnp.sum(before_me * takes_int[None, :], axis=1),
        jnp.sum(takes_int) + jnp.sum(before_me * (1 - takes_int)[None, :], axis=1),
    )
    wanted = jnp.minimum(spots, number - 1)
    order = jnp.sum(jnp.where(rank[None, :] == wanted[:, None], spots[None, :], 0), axis=1)
    order = jnp.concatenate([order, number[None]]).astype(jnp.int32)

    def constant(table):
        return pl.BlockSpec(table.shape, lambda i, g, *_: (0, 0))

    def page(i, g, scal, order):
        return (order[g], i, 0, 0)

    rest = SHARED_C - SHARED_D
    c6, c6_rest, ahead_row, d6, d6_self = values[:5]
    operands = [c6, c6, c6_rest, c6_rest, ahead_row, d6, d6_self]
    following = lambda i: jnp.minimum((i + 1) // 2, half_rows - 1)
    in_specs = [
        rest_spec(SHARED_D, lambda i: i // 2),
        rest_spec(SHARED_D, following),
        rest_spec(rest, lambda i: i // 2),
        rest_spec(rest, following),
        rest_spec(SHARED_C, lambda i: 0),
        rest_spec(SHARED_D, lambda i: i // 2),
        rest_spec(rest, lambda i: i // 2),
    ]
    aliases = {}
    if not fine:
        c5, c5_low, c5_high, s5_self = values[5:]
        operands += [c5[slot] for slot in SLOTS] + [c5_low, c5_high, s5_self]
        in_specs += [
            pl.BlockSpec((SHARED_D, 1, QR, HALF_LANES), lambda i, g, *_: (0, i, 0, 0))
        ] * 8 + [
            rest_spec(rest, lambda i: jnp.minimum(i, half_rows - 1)),
            rest_spec(rest, lambda i: jnp.maximum(i - half_rows, 0)),
            line_spec(lambda i: i),
        ]
        c4 = jnp.stack([c5[slot][SHARED_D] for slot in SLOTS])
        operands += [c4.reshape((2, 2, 2) + c4.shape[1:]), before]
        in_specs += [line_spec(lambda i: i), pl.BlockSpec(memory_space=pl.ANY)]
        aliases = {2 + len(operands) - 1: 0}
    return pl.pallas_call(
        lambda *refs: backward_kernel(fine, rows_here, count, *refs),
        grid_spec=pltpu.PrefetchScalarGridSpec(
            num_scalar_prefetch=2,
            grid=(rows_here, count),
            in_specs=in_specs + [constant(table) for table in ordered],
            out_specs=pl.BlockSpec((1, 1, N2, N3 * N4), page),
            scratch_shapes=[
                pltpu.VMEM((4, GROUPS, HB + QR, TILE), jnp.float32),
                pltpu.VMEM((4, GROUPS, HB, TILE), jnp.float32),
                pltpu.VMEM((GROUPS, N2, TILE), jnp.float32),
                pltpu.VMEM((GROUPS, N2, 12 * TILE), jnp.bfloat16),
            ],
        ),
        out_shape=jax.ShapeDtypeStruct((count, rows_here, N2, N3 * N4), jnp.float32),
        input_output_aliases=aliases,
        compiler_params=pltpu.CompilerParams(vmem_limit_bytes=60 * 2**20),
        cost_estimate=pl.CostEstimate(
            flops=10**10, bytes_accessed=60 * 2**20, transcendentals=0
        ),
        name="join_fine" if fine else "join_coarse",
    )(scal, order, *operands, *ordered)


def stack_slots(pieces):
    return jnp.stack(
        [
            jnp.stack([jnp.stack([pieces[h, sx, sy] for sy in range(2)]) for sx in range(2)])
            for h in range(2)
        ]
    )


def exchange(value, axis, domains):
    dom_count = lax.axis_size("dom")
    pairs = []
    for x in range(2):
        for y in range(2):
            other = (1 - x, y) if axis == "half" else (x, 1 - y)
            for d in range(domains):
                pairs.append(
                    ((x * 2 + y) * dom_count + d, (other[0] * 2 + other[1]) * dom_count + d)
                )
    return lax.ppermute(value, ("half", "grid", "dom"), pairs)


def reduce_quarter(pieces, domains):
    reduced = []
    for h in range(2):
        first, second = (("half", "grid"), ("grid", "half"))[h]
        far = lambda a, b: pieces[(h, a, b) if h == 0 else (h, b, a)]
        onward = exchange(far(1, 1), first, domains)
        nearby = exchange(far(1, 0), first, domains)
        onward = far(0, 1) + onward
        nearby = far(0, 0) + nearby
        reduced.append(nearby + exchange(onward, second, domains))
    return jnp.stack(reduced)


def gather_quarters(own, domains):
    pieces = {}
    for h in range(2):
        first, second = (("half", "grid"), ("grid", "half"))[h]
        place = lambda a, b: (h, a, b) if h == 0 else (h, b, a)
        pieces[place(0, 0)] = own[h]
        pieces[place(0, 1)] = exchange(own[h], second, domains)
        pieces[place(1, 0)] = exchange(own[h], first, domains)
        pieces[place(1, 1)] = exchange(pieces[place(0, 1)], first, domains)
    return pieces


def rows_up(value, sources):
    half_rows = value.shape[-3] // 2
    low = lax.ppermute(value[..., :half_rows, :, :], "dom", [(d, 2 * d) for d in range(sources)])
    high = lax.ppermute(
        value[..., half_rows:, :, :], "dom", [(d, 2 * d + 1) for d in range(sources)]
    )
    return low + high


def rows_down(value):
    targets = lax.axis_size("dom") // 2
    low = lax.ppermute(value, "dom", [(2 * d, d) for d in range(targets)])
    high = lax.ppermute(value, "dom", [(2 * d + 1, d) for d in range(targets)])
    return jnp.concatenate([low, high], axis=-3)


def next_row(value, devices):
    return lax.ppermute(
        value[..., :1, :, :], "dom", [((d + 1) % devices, d) for d in range(devices)]
    )


def per_device(grids, levels):
    count, rows_here = grids.shape[:2]
    half_rows = rows_here // 2
    half_size = lax.axis_size("half")
    grid_size = lax.axis_size("grid")
    dom_size = lax.axis_size("dom")
    square = half_size == 2 and grid_size == 2
    group = lax.axis_index("half") * grid_size + lax.axis_index("grid")
    weights = combination_weights(levels).astype(jnp.float32)
    lowest = jnp.array(
        [LEV1 - SPANS[0], LEV2 - SPANS[1], LEV3 - SPANS[2], LEV4 - SPANS[3]], dtype=jnp.int32
    )
    offsets = levels - lowest[None, :]
    own_offsets = lax.dynamic_slice_in_dim(offsets, group * count, count, 0)
    own_weights = lax.dynamic_slice_in_dim(weights, group * count, count, 0)
    zero = jnp.zeros((), jnp.int32)
    place = jnp.stack(
        [
            lax.axis_index("half") if square else zero,
            lax.axis_index("grid") if square else zero,
            lax.axis_index("dom") * rows_here,
        ]
    ).astype(jnp.int32)
    scal = jnp.concatenate([own_offsets.reshape(-1), place])
    sources = dom_size // 2
    quarter_devices = dom_size // 4
    s4 = coarsest(grids, scal, own_weights)[:, :, :, None]
    ahead = next_row(s4, quarter_devices)
    longer = jnp.concatenate([s4, ahead], axis=-3)
    mids = 0.5 * (longer[..., :-1, :, :] + longer[..., 1:, :, :])
    spread = jnp.stack([s4, mids], axis=-3).reshape(
        s4.shape[:-3] + (2 * rows_here,) + s4.shape[-2:]
    )
    spread = rows_up(spread, quarter_devices)
    coarsest_rows = rows_up(spread, sources)

    coarse_parts = forward(False, grids, scal, own_weights)
    s5 = dict(zip(SLOTS, coarse_parts[:8]))
    s5_low, s5_high, s5_self = coarse_parts[8:]
    fine_parts = forward(True, grids, scal, own_weights)
    e6 = dict(zip(SLOTS, fine_parts[:8]))
    d6 = dict(zip(SLOTS, fine_parts[8:16]))
    e6_rest, d6_self = fine_parts[16:]

    from_low = lax.ppermute(s5_low, "dom", [(d, 2 * d) for d in range(sources)])
    from_high = lax.ppermute(s5_high, "dom", [(d, 2 * d + 1) for d in range(sources)])
    c6_rest = e6_rest + from_low + from_high
    firsts = jnp.concatenate(
        [stack_slots({slot: e6[slot][:, :1] for slot in SLOTS}), e6_rest[..., :1, :, :]], axis=3
    )
    e6_ahead = next_row(firsts, dom_size)
    d6_self = d6_self.at[..., -1:, :, :].add(-0.5 * e6_ahead[:, :, :, SHARED_D:])
    d6 = {
        slot: d6[slot].at[:, -1:].add(-0.5 * e6_ahead[slot][:SHARED_D]) for slot in SLOTS
    }

    e6 = {slot: e6[slot].at[:1].add(coarsest_rows[slot]) for slot in SLOTS}

    if square:
        s5_own = reduce_quarter(s5, sources)
        d6_own = reduce_quarter(d6, dom_size)
        e6_own = reduce_quarter(e6, dom_size)
        rest_own = reduce_quarter({slot: c6_rest[slot] for slot in SLOTS}, dom_size)
    else:
        s5_own, e6_own, d6_own, rest_own = lax.psum(
            (stack_slots(s5), stack_slots(e6), stack_slots(d6), c6_rest), ("half", "grid")
        )
    c6_own = e6_own + rows_up(s5_own, sources)
    c5_own = rows_down(c6_own)
    if half_rows > 1:
        pieces = [
            lax.ppermute(
                c6_own[..., :1, ::2, :, :], "dom", [(4 * d + r, d) for d in range(quarter_devices)]
            )
            for r in range(4)
        ]
    else:
        pieces = [
            lax.ppermute(
                c6_own[..., :1, :, :, :], "dom", [(4 * d + r, d) for d in range(quarter_devices)]
            )
            for r in (0, 2)
        ]
    c4_own = jnp.concatenate(pieces, axis=-3)
    c5_own = jnp.concatenate([c5_own, c4_own], axis=-4)
    ahead_own = next_row(
        jnp.concatenate([c6_own[..., :1, :, :], rest_own[..., :1, :, :]], axis=-4), dom_size
    )
    if square:
        d6 = stack_slots(gather_quarters(d6_own, dom_size))
        c6_rest = stack_slots(gather_quarters(rest_own, dom_size))
        c6 = stack_slots(gather_quarters(c6_own, dom_size))
        ahead_row = stack_slots(gather_quarters(ahead_own, dom_size))
        c5 = gather_quarters(c5_own, sources)
    else:
        c6, d6, c6_rest, ahead_row = c6_own, d6_own, rest_own, ahead_own
        c5 = {slot: c5_own[slot] for slot in SLOTS}
    c5_low = lax.ppermute(c6_rest, "dom", [(2 * d, d) for d in range(sources)])
    c5_high = lax.ppermute(c6_rest, "dom", [(2 * d + 1, d) for d in range(sources)])
    values = [c6, c6_rest, ahead_row, d6, d6_self]
    written = backward(True, count, scal, rows_here, values)
    values += [c5, c5_low, c5_high, s5_self]
    return backward(False, count, scal, rows_here, values, written)


def solution(mesh):
    return jax.shard_map(
        per_device,
        mesh=mesh,
        in_specs=(P(("half", "grid"), "dom", None, None), P()),
        out_specs=P(("half", "grid"), "dom", None, None),
        check_vma=False,
    )
```

```python
import jax
import jax.numpy as jnp
import numpy as np
from jax import lax
from jax.experimental import pallas as pl
from jax.experimental.pallas import tpu as pltpu
from jax.sharding import PartitionSpec as P


LEV1 = 6
LEV2 = 6
LEV3 = 6
LEV4 = 6
N1 = 64
N2 = 64
N3 = 64
N4 = 64
SPANS = (2, 1, 1, 1)


BLOCKS = (
    (0, 0, 0), (1, 0, 0), (0, 1, 0), (0, 0, 1),
    (1, 1, 0), (1, 0, 1), (0, 1, 1), (1, 1, 1),
)
SHARED_D = 4
SHARED_C = 7
HB = N2 // 2
HC = N3 // 2
HD = N4 // 2
GROUPS = 8
CG = N3 // GROUPS
LANES = HC * HD
HALF_LANES = LANES // 2
QR = HB // 4
TILE = CG // 2 * HD
SLOTS = tuple((h, sx, sy) for h in range(2) for sx in range(2) for sy in range(2))


def combination_weights(levels):
    corners = np.array(
        [[corner >> place & 1 for place in range(4)] for corner in range(16)], dtype=np.int32
    )
    parity = 1 - 2 * (corners.sum(axis=1) % 2)
    raised = levels[:, None, :] + jnp.asarray(corners, dtype=jnp.int32)[None, :, :]
    below = jnp.all(raised[:, :, None, :] <= levels[None, None, :, :], axis=3)
    inside = jnp.any(below, axis=2).astype(jnp.int32)
    return jnp.sum(inside * jnp.asarray(parity, dtype=jnp.int32)[None, :], axis=1)


def split_matrix(count_in, half, wrap):
    table = np.zeros((count_in, 2, half))
    for k in range(half):
        table[2 * k, 0, k] = 1.0
        table[2 * k + 1, 1, k] += 1.0
        table[2 * k, 1, k] -= 0.5
        table[(2 * k + 2) % wrap, 1, k] -= 0.5
    return table


def plain_matrix(count_in, half):
    table = np.zeros((count_in, 1, half))
    for k in range(half):
        table[k, 0, k] = 1.0
    return table


def join_matrix(parts_in, half_out, wrap, next_points):
    table = np.zeros((parts_in, half_out + next_points, 2 * half_out))
    for k in range(half_out):
        table[0, k, 2 * k] = 1.0
        table[1, k, 2 * k + 1] += 1.0
        table[0, k, 2 * k + 1] += 0.5
        table[0, (k + 1) % wrap, 2 * k + 1] += 0.5
    return table


def forward_tables():
    half_c = CG // 2
    tables = {}
    for oc in range(2):
        for od in range(2):
            if oc:
                along_c = split_matrix(CG + 2, half_c, CG + 2)
            else:
                along_c = plain_matrix(half_c, half_c)
            along_d = split_matrix(N4, HD, N4) if od else plain_matrix(N4, HD)
            table = np.einsum("cpk,dql->cdpqkl", along_c, along_d)
            rows = along_c.shape[0] * N4
            tables[oc, od] = jnp.asarray(table.reshape(rows, -1), jnp.bfloat16)
    return tables


def backward_tables():
    half_c = CG // 2
    tables = {}
    for oc in range(2):
        for od in range(2):
            if od:
                along_d = join_matrix(2, HD, HD, 0)
            else:
                along_d = np.zeros((1, HD, N4))
                along_d[0, np.arange(HD), np.arange(HD)] = 1.0
            if oc:
                along_c = join_matrix(2, half_c, half_c + half_c, half_c)
                own = np.einsum("pkc,qld->pqklcd", along_c[:, :half_c], along_d)
                ahead = np.einsum("pkc,qld->pqklcd", along_c[:1, half_c:], along_d)
                cols = CG * N4
                table = np.concatenate([own.reshape(-1, cols), ahead.reshape(-1, cols)], axis=0)
            else:
                along_c = np.eye(half_c)[None]
                table = np.einsum("pkc,qld->pqklcd", along_c, along_d).reshape(-1, half_c * N4)
            tables[oc, od] = jnp.asarray(table, jnp.bfloat16)
    return tables


CASES = ((0, 0), (0, 1), (1, 0), (1, 1))


def split_parts(value):
    high = value.astype(jnp.bfloat16)
    low = (value - high.astype(jnp.float32)).astype(jnp.bfloat16)
    return high, low


def grid_facts(scal, g):
    return tuple(scal[4 * g + axis] for axis in range(4))


def forward_kernel(rows_here, count, scal, fetch, weight, x_ref, *refs):
    tables = dict(zip(CASES, refs[:4]))
    outs = refs[5:-2]
    xb, yb = refs[-2:]
    half_rows = rows_here // 2
    i = pl.program_id(0)
    g = pl.program_id(1)
    level, fine_b, fine_c, fine_d = grid_facts(scal, g)
    mine_x = scal[4 * count]
    mine_y = scal[4 * count + 1]
    row = scal[4 * count + 2] + i
    odd = lax.rem(i, 2) == 1
    even = lax.rem(i, 2) == 0
    active = row < (N1 // 4) * (1 << level)
    active = active & (level > 0)

    def clear(wanted, *targets):
        @pl.when((g == 0) & wanted)
        def _():
            for target in targets:
                target[...] = jnp.zeros_like(target)

    s5 = dict(zip(SLOTS, outs[:8]))
    s5_low, s5_high, s5_self = outs[8:11]
    e6 = dict(zip(SLOTS, outs[11:19]))
    d6 = dict(zip(SLOTS, outs[19:27]))
    e6_rest, d6_self = outs[27:]
    clear(i >= 0, *outs[:8], s5_self)
    clear(i < half_rows, s5_low)
    clear(i >= half_rows, s5_high)
    clear(even, *outs[11:19], e6_rest)
    clear(odd, *outs[19:27], d6_self)

    def put(row_count, fine_c_here):
        rows = slice(0, row_count)
        span = CG * N4 if fine_c_here else CG // 2 * N4
        reach = span + 2 * N4 if fine_c_here else span
        for k in range(GROUPS):
            for lane in range(0, span, 2 * N4):
                value = x_ref[0, 0, rows, k * span + lane : k * span + lane + 2 * N4]
                for place, piece in zip((0, reach), split_parts(value)):
                    xb[k, rows, place + lane : place + lane + 2 * N4] = piece
                    if fine_c_here and lane == 0:
                        before = (k + GROUPS - 1) % GROUPS
                        xb[before, rows, place + span : place + reach] = piece

    for oc, od in CASES:
        for ob in range(2):
            @pl.when(active & (fine_b == ob) & (fine_c == oc) & (fine_d == od))
            def _(oc=oc, od=od, ob=ob):
                rows = (1 + ob) * HB
                put(rows, oc)
                reach = (CG + 2) * N4 if oc else CG // 2 * N4
                table = tables[oc, od][...]
                lhs = xb[:, :rows, : 2 * reach].reshape(GROUPS * rows, 2 * reach)
                result = jnp.dot(
                    lhs[:, :reach], table, preferred_element_type=jnp.float32
                ) + jnp.dot(lhs[:, reach:], table, preferred_element_type=jnp.float32)
                for pc in range(oc + 1):
                    for pd in range(od + 1):
                        column = (pc * (od + 1) + pd) * TILE
                        for k in range(GROUPS):
                            piece = result[k * rows : k * rows + rows, column : column + TILE]
                            if ob:
                                yb[2 * pc + pd, k, :N2] = piece
                                yb[2 * pc + pd, k, N2:] = piece[:QR]
                            else:
                                yb[2 * pc + pd, k, pl.ds(0, HB, stride=2)] = piece

    scale = weight[g]

    def add_up(wanted, blocks, target):
        for block in blocks:
            pb, pc, pd = BLOCKS[block]

            @pl.when(wanted & (pb <= fine_b) & (pc <= fine_c) & (pd <= fine_d))
            def _(block=block, pb=pb, part=2 * pc + pd):
                for h, sx, sy in SLOTS:
                    quarter = 2 * (sx ^ mine_x) + (sy ^ mine_y)
                    start = pl.multiple_of(quarter * 2 * QR, 2 * QR)
                    ref, index = target(block, h, sx, sy)
                    for j in range(GROUPS // 2):
                        k = h * (GROUPS // 2) + j
                        piece = yb[part, k, pl.ds(start, QR, stride=2)]
                        if pb:
                            piece = yb[part, k, pl.ds(start + 1, QR, stride=2)] - 0.5 * (
                                piece + yb[part, k, pl.ds(start + 2, QR, stride=2)]
                            )
                        where = index + (slice(None), slice(j * TILE, j * TILE + TILE))
                        ref[where] += scale * piece

    def slot_of(parts):
        return lambda block, h, sx, sy: (parts[h, sx, sy], (block, 0))

    def rest_of(ref):
        return lambda block, h, sx, sy: (ref, (h, sx, sy, block - SHARED_D, 0))

    def line_of(ref):
        return lambda block, h, sx, sy: (ref, (h, sx, sy, 0))

    six = active & (level == 2)
    five = active & (level == 1)
    add_up(six & even, range(SHARED_D), slot_of(e6))
    add_up(six & even, range(SHARED_D, SHARED_C), rest_of(e6_rest))
    add_up(six & odd, range(SHARED_D), slot_of(d6))
    add_up(six & odd, range(SHARED_D, SHARED_C), rest_of(d6_self))
    add_up(five, range(SHARED_D), slot_of(s5))
    add_up(five & (i < half_rows), range(SHARED_D, SHARED_C), rest_of(s5_low))
    add_up(five & (i >= half_rows), range(SHARED_D, SHARED_C), rest_of(s5_high))
    add_up(five, range(SHARED_C, 8), line_of(s5_self))

    @pl.when((g == count - 1) & (i > 0))
    def _():
        for slot in SLOTS:
            d6[slot][...] -= 0.5 * e6[slot][...]
        d6_self[...] -= 0.5 * e6_rest[...]


def forward(grids, scal, weight, after):
    count, rows_here = grids.shape[:2]
    half_rows = rows_here // 2
    tables = forward_tables()
    levels = scal[: 4 * count].reshape(count, 4)[:, 0]
    rows = scal[4 * count + 2] + jnp.arange(rows_here, dtype=jnp.int32)
    takes = (levels > 0)[None, :] & (rows[:, None] < (N1 // 4) * (1 << levels)[None, :])
    steps = jnp.arange(rows_here * count, dtype=jnp.int32)
    earlier = (steps[None, :] <= steps[:, None]) & takes.reshape(-1)[None, :]
    fetch = jnp.max(jnp.where(earlier, steps[None, :], 0), axis=1)

    def constant(table):
        return pl.BlockSpec(table.shape, lambda i, g, *_: (0, 0))

    def page(i, g, scal, fetch, weight):
        step = fetch[i * count + g]
        return (lax.rem(step, count), step // count, 0, 0)

    def rows_spec(blocks, row_of):
        return pl.BlockSpec(
            (blocks, 1, QR, HALF_LANES), lambda i, g, *_: (0, row_of(i), 0, 0)
        )

    def shape(*dims):
        return jax.ShapeDtypeStruct(dims + (QR, HALF_LANES), jnp.float32)

    def even_row(i):
        return i // 2

    def odd_row(i):
        return jnp.maximum(i - 1, 0) // 2

    rest = SHARED_C - SHARED_D
    out_specs = (
        [rows_spec(SHARED_D, lambda i: i)] * 8
        + [
            rest_spec(rest, lambda i: jnp.minimum(i, half_rows - 1)),
            rest_spec(rest, lambda i: jnp.maximum(i - half_rows, 0)),
            line_spec(lambda i: i),
        ]
        + [rows_spec(SHARED_D, even_row)] * 8
        + [rows_spec(SHARED_D, odd_row)] * 8
        + [rest_spec(rest, even_row), rest_spec(rest, odd_row)]
    )
    out_shape = (
        [shape(SHARED_D, rows_here)] * 8
        + [shape(2, 2, 2, rest, half_rows)] * 2
        + [shape(2, 2, 2, rows_here)]
        + [shape(SHARED_D, half_rows)] * 16
        + [shape(2, 2, 2, rest, half_rows)] * 2
    )
    ordered = [tables[case] for case in CASES]
    return pl.pallas_call(
        lambda *refs: forward_kernel(rows_here, count, *refs),
        grid_spec=pltpu.PrefetchScalarGridSpec(
            num_scalar_prefetch=3,
            grid=(rows_here, count),
            in_specs=[pl.BlockSpec((1, 1, N2, N3 * N4), page)]
            + [constant(table) for table in ordered]
            + [pl.BlockSpec(memory_space=pl.ANY)],
            out_specs=out_specs,
            scratch_shapes=[
                pltpu.VMEM((GROUPS, 2 * HB, 2 * (CG + 2) * N4), jnp.bfloat16),
                pltpu.VMEM((4, GROUPS, N2 + QR, TILE), jnp.float32),
            ],
        ),
        out_shape=out_shape,
        compiler_params=pltpu.CompilerParams(vmem_limit_bytes=60 * 2**20),
        cost_estimate=pl.CostEstimate(
            flops=10**10, bytes_accessed=60 * 2**20, transcendentals=0
        ),
        name="split_grids",
    )(scal, fetch, weight, grids, *ordered, after)


def coarsest_kernel(count, scal, weight, x_ref, table, out, yb):
    i = pl.program_id(0)
    mine_x = scal[4 * count]
    mine_y = scal[4 * count + 1]
    g = scal[4 * count + 3]
    active = (scal[4 * g] == 0) & (scal[4 * count + 2] + i < N1 // 4)

    @pl.when(jnp.logical_not(active))
    def _():
        out[...] = jnp.zeros_like(out)

    @pl.when(active)
    def _():
        span = CG // 2 * N4
        for k in range(GROUPS):
            high, low = split_parts(x_ref[0, 0, :, k * span : k * span + span])
            yb[k] = weight[g] * (
                jnp.dot(high, table[...], preferred_element_type=jnp.float32)
                + jnp.dot(low, table[...], preferred_element_type=jnp.float32)
            )
        for h, sx, sy in SLOTS:
            quarter = 2 * (sx ^ mine_x) + (sy ^ mine_y)
            start = pl.multiple_of(quarter * QR, QR)
            for j in range(GROUPS // 2):
                out[h, sx, sy, 0, :, j * TILE : j * TILE + TILE] = yb[
                    h * (GROUPS // 2) + j, pl.ds(start, QR)
                ]


def coarsest(grids, scal, weight):
    count, rows_here = grids.shape[:2]
    table = forward_tables()[0, 0]

    def page(i, scal, weight):
        g = scal[4 * count + 3]
        wanted = (scal[4 * g] == 0) & (scal[4 * count + 2] + i < N1 // 4)
        return (g, jnp.where(wanted, i, 0), 0, 0)

    return pl.pallas_call(
        lambda *refs: coarsest_kernel(count, *refs),
        grid_spec=pltpu.PrefetchScalarGridSpec(
            num_scalar_prefetch=2,
            grid=(rows_here,),
            in_specs=[
                pl.BlockSpec((1, 1, HB, HC * N4), page),
                pl.BlockSpec(table.shape, lambda i, *_: (0, 0)),
            ],
            out_specs=line_spec(lambda i: i),
            scratch_shapes=[pltpu.VMEM((GROUPS, HB, TILE), jnp.float32)],
        ),
        out_shape=jax.ShapeDtypeStruct((2, 2, 2, rows_here, QR, HALF_LANES), jnp.float32),
        compiler_params=pltpu.CompilerParams(vmem_limit_bytes=60 * 2**20),
        cost_estimate=pl.CostEstimate(
            flops=10**8, bytes_accessed=4 * 2**20, transcendentals=0
        ),
        name="split_coarsest",
    )(scal, weight, grids, table)


def rest_spec(blocks, row_of):
    return pl.BlockSpec(
        (2, 2, 2, blocks, 1, QR, HALF_LANES), lambda i, g, *_: (0, 0, 0, 0, row_of(i), 0, 0)
    )


def line_spec(row_of):
    return pl.BlockSpec(
        (2, 2, 2, 1, QR, HALF_LANES), lambda i, *_: (0, 0, 0, row_of(i), 0, 0)
    )


def backward_kernel(rows_here, count, scal, *refs):
    used = 19
    c6, c6_next, c6_rest, c6_rest_next, ahead_row, d6, d6_self = refs[:7]
    c5 = dict(zip(SLOTS, refs[7:15]))
    c5_low, c5_high, s5_self, c4 = refs[15:19]
    tables = dict(zip(CASES, refs[used : used + 4]))
    out = refs[used + 4]
    coarse, detail, joined, xb = refs[used + 5 :]
    half_rows = rows_here // 2
    i = pl.program_id(0)
    g = pl.program_id(1)
    level, fine_b, fine_c, fine_d = grid_facts(scal, g)
    mine_x = scal[4 * count]
    mine_y = scal[4 * count + 1]
    row = scal[4 * count + 2] + i
    odd = lax.rem(i, 2) == 1
    even = lax.rem(i, 2) == 0
    active = row < (N1 // 4) * (1 << level)

    def stage(wanted, blocks, source):
        for block in blocks:
            pb, pc, pd = BLOCKS[block]

            @pl.when(active & wanted & (pb <= fine_b) & (pc <= fine_c) & (pd <= fine_d))
            def _(block=block, work=(coarse, detail)[pb], part=2 * pc + pd):
                for h, sx, sy in SLOTS:
                    quarter = 2 * (sx ^ mine_x) + (sy ^ mine_y)
                    start = pl.multiple_of(quarter * QR, QR)
                    value = source(block, h, sx, sy)
                    for j in range(GROUPS // 2):
                        k = h * (GROUPS // 2) + j
                        work[part, k, pl.ds(start, QR)] = value[:, j * TILE : j * TILE + TILE]

    def here(block, h, sx, sy):
        if block < SHARED_D:
            return c6[h, sx, sy, block, 0]
        return c6_rest[h, sx, sy, block - SHARED_D, 0]

    def between(last):
        def value(block, h, sx, sy):
            if last:
                after = ahead_row[h, sx, sy, block, 0]
            elif block < SHARED_D:
                after = c6_next[h, sx, sy, block, 0]
            else:
                after = c6_rest_next[h, sx, sy, block - SHARED_D, 0]
            mean = 0.5 * (here(block, h, sx, sy) + after)
            if block < SHARED_D:
                return mean + d6[h, sx, sy, block, 0]
            return mean + d6_self[h, sx, sy, block - SHARED_D, 0]

        return value

    stage((level == 2) & even, range(SHARED_C), here)
    if half_rows > 1:
        stage((level == 2) & odd & (i < rows_here - 1), range(SHARED_C), between(False))
    stage((level == 2) & odd & (i == rows_here - 1), range(SHARED_C), between(True))
    rest = range(SHARED_D, SHARED_C)
    five = level == 1
    stage(five, range(SHARED_D), lambda b, h, x, y: c5[h, x, y][b, 0])
    stage(five & (i < half_rows), rest, lambda b, h, x, y: c5_low[h, x, y, b - SHARED_D, 0])
    stage(five & (i >= half_rows), rest, lambda b, h, x, y: c5_high[h, x, y, b - SHARED_D, 0])
    stage(five, range(SHARED_C, 8), lambda b, h, x, y: s5_self[h, x, y, 0])
    stage(level == 0, range(1), lambda b, h, x, y: c4[h, x, y, 0])

    @pl.when(jnp.logical_not(active))
    def _():
        out[...] = jnp.zeros_like(out)

    for oc, od in CASES:
        for ob in range(2):
            @pl.when(active & (fine_b == ob) & (fine_c == oc) & (fine_d == od))
            def _(oc=oc, od=od, ob=ob):
                parts = [(pc, pd) for pc in range(oc + 1) for pd in range(od + 1)]
                ahead = [(0, pd) for pd in range(od + 1)] if oc else []
                reach = (len(parts) + len(ahead)) * TILE
                rows = (1 + ob) * HB
                for place, (pc, pd) in enumerate(parts):
                    part = 2 * pc + pd
                    for k in range(GROUPS):
                        value = coarse[part, k, :HB]
                        if ob:
                            coarse[part, k, HB:] = coarse[part, k, :QR]
                            mean = 0.5 * (value + coarse[part, k, 1 : HB + 1])
                            joined[k, pl.ds(0, HB, stride=2)] = value
                            joined[k, pl.ds(1, HB, stride=2)] = detail[part, k] + mean
                            value = joined[k]
                        for base, piece in zip((0, reach), split_parts(value)):
                            start = base + place * TILE
                            xb[k, :rows, start : start + TILE] = piece
                            if oc and not pc:
                                start = base + (len(parts) + pd) * TILE
                                before = (k + GROUPS - 1) % GROUPS
                                xb[before, :rows, start : start + TILE] = piece
                table = tables[oc, od][...]
                lhs = xb[:, :rows, : 2 * reach].reshape(GROUPS * rows, 2 * reach)
                result = jnp.dot(
                    lhs[:, :reach], table, preferred_element_type=jnp.float32
                ) + jnp.dot(lhs[:, reach:], table, preferred_element_type=jnp.float32)
                span = CG * N4 if oc else CG // 2 * N4
                for k in range(GROUPS):
                    out[0, 0, :rows, k * span : k * span + span] = result[
                        k * rows : k * rows + rows
                    ]
                if not ob:
                    out[0, 0, HB:, :] = jnp.zeros((HB, N3 * N4), jnp.float32)
                if not oc:
                    out[0, 0, :, HC * N4 :] = jnp.zeros((N2, HC * N4), jnp.float32)


def backward(count, scal, rows_here, values):
    half_rows = rows_here // 2
    tables = backward_tables()
    ordered = [tables[case] for case in CASES]

    def constant(table):
        return pl.BlockSpec(table.shape, lambda i, g, *_: (0, 0))

    rest = SHARED_C - SHARED_D
    c6, c6_rest, ahead_row, d6, d6_self = values[:5]
    operands = [c6, c6, c6_rest, c6_rest, ahead_row, d6, d6_self]
    following = lambda i: jnp.minimum((i + 1) // 2, half_rows - 1)
    in_specs = [
        rest_spec(SHARED_D, lambda i: i // 2),
        rest_spec(SHARED_D, following),
        rest_spec(rest, lambda i: i // 2),
        rest_spec(rest, following),
        rest_spec(SHARED_C, lambda i: 0),
        rest_spec(SHARED_D, lambda i: i // 2),
        rest_spec(rest, lambda i: i // 2),
    ]
    c5, c5_low, c5_high, s5_self = values[5:]
    operands += [c5[slot] for slot in SLOTS] + [c5_low, c5_high, s5_self]
    in_specs += [
        pl.BlockSpec((SHARED_D, 1, QR, HALF_LANES), lambda i, g, *_: (0, i, 0, 0))
    ] * 8 + [
        rest_spec(rest, lambda i: jnp.minimum(i, half_rows - 1)),
        rest_spec(rest, lambda i: jnp.maximum(i - half_rows, 0)),
        line_spec(lambda i: i),
    ]
    c4 = jnp.stack([c5[slot][SHARED_D] for slot in SLOTS])
    operands.append(c4.reshape((2, 2, 2) + c4.shape[1:]))
    in_specs.append(line_spec(lambda i: i))
    return pl.pallas_call(
        lambda *refs: backward_kernel(rows_here, count, *refs),
        grid_spec=pltpu.PrefetchScalarGridSpec(
            num_scalar_prefetch=1,
            grid=(rows_here, count),
            in_specs=in_specs + [constant(table) for table in ordered],
            out_specs=pl.BlockSpec((1, 1, N2, N3 * N4), lambda i, g, *_: (g, i, 0, 0)),
            scratch_shapes=[
                pltpu.VMEM((4, GROUPS, HB + QR, TILE), jnp.float32),
                pltpu.VMEM((4, GROUPS, HB, TILE), jnp.float32),
                pltpu.VMEM((GROUPS, N2, TILE), jnp.float32),
                pltpu.VMEM((GROUPS, N2, 12 * TILE), jnp.bfloat16),
            ],
        ),
        out_shape=jax.ShapeDtypeStruct((count, rows_here, N2, N3 * N4), jnp.float32),
        compiler_params=pltpu.CompilerParams(vmem_limit_bytes=60 * 2**20),
        cost_estimate=pl.CostEstimate(
            flops=10**10, bytes_accessed=60 * 2**20, transcendentals=0
        ),
        name="join_grids",
    )(scal, *operands, *ordered)


def stack_slots(pieces):
    return jnp.stack(
        [
            jnp.stack([jnp.stack([pieces[h, sx, sy] for sy in range(2)]) for sx in range(2)])
            for h in range(2)
        ]
    )


def exchange(value, axis, domains):
    dom_count = lax.axis_size("dom")
    pairs = []
    for x in range(2):
        for y in range(2):
            other = (1 - x, y) if axis == "half" else (x, 1 - y)
            for d in range(domains):
                pairs.append(
                    ((x * 2 + y) * dom_count + d, (other[0] * 2 + other[1]) * dom_count + d)
                )
    return lax.ppermute(value, ("half", "grid", "dom"), pairs)


def reduce_quarter(pieces, domains):
    reduced = []
    for h in range(2):
        first, second = (("half", "grid"), ("grid", "half"))[h]
        far = lambda a, b: pieces[(h, a, b) if h == 0 else (h, b, a)]
        onward = exchange(far(1, 1), first, domains)
        nearby = exchange(far(1, 0), first, domains)
        onward = far(0, 1) + onward
        nearby = far(0, 0) + nearby
        reduced.append(nearby + exchange(onward, second, domains))
    return jnp.stack(reduced)


def gather_quarters(own, domains):
    pieces = {}
    for h in range(2):
        first, second = (("half", "grid"), ("grid", "half"))[h]
        place = lambda a, b: (h, a, b) if h == 0 else (h, b, a)
        pieces[place(0, 0)] = own[h]
        pieces[place(0, 1)] = exchange(own[h], second, domains)
        pieces[place(1, 0)] = exchange(own[h], first, domains)
        pieces[place(1, 1)] = exchange(pieces[place(0, 1)], first, domains)
    return pieces


def rows_up(value, sources):
    half_rows = value.shape[-3] // 2
    low = lax.ppermute(value[..., :half_rows, :, :], "dom", [(d, 2 * d) for d in range(sources)])
    high = lax.ppermute(
        value[..., half_rows:, :, :], "dom", [(d, 2 * d + 1) for d in range(sources)]
    )
    return low + high


def rows_down(value):
    targets = lax.axis_size("dom") // 2
    low = lax.ppermute(value, "dom", [(2 * d, d) for d in range(targets)])
    high = lax.ppermute(value, "dom", [(2 * d + 1, d) for d in range(targets)])
    return jnp.concatenate([low, high], axis=-3)


def next_row(value, devices):
    return lax.ppermute(
        value[..., :1, :, :], "dom", [((d + 1) % devices, d) for d in range(devices)]
    )


def per_device(grids, levels):
    count, rows_here = grids.shape[:2]
    half_rows = rows_here // 2
    half_size = lax.axis_size("half")
    grid_size = lax.axis_size("grid")
    dom_size = lax.axis_size("dom")
    square = half_size == 2 and grid_size == 2
    group = lax.axis_index("half") * grid_size + lax.axis_index("grid")
    weights = combination_weights(levels).astype(jnp.float32)
    lowest = jnp.array(
        [LEV1 - SPANS[0], LEV2 - SPANS[1], LEV3 - SPANS[2], LEV4 - SPANS[3]], dtype=jnp.int32
    )
    offsets = levels - lowest[None, :]
    own_offsets = lax.dynamic_slice_in_dim(offsets, group * count, count, 0)
    own_weights = lax.dynamic_slice_in_dim(weights, group * count, count, 0)
    zero = jnp.zeros((), jnp.int32)
    place = jnp.stack(
        [
            lax.axis_index("half") if square else zero,
            lax.axis_index("grid") if square else zero,
            lax.axis_index("dom") * rows_here,
        ]
    ).astype(jnp.int32)
    first = jnp.argmax(own_offsets[:, 0] == 0).astype(jnp.int32)
    scal = jnp.concatenate([own_offsets.reshape(-1), place, first[None]])
    sources = dom_size // 2
    quarter_devices = dom_size // 4
    s4 = coarsest(grids, scal, own_weights)[:, :, :, None]
    ahead = next_row(s4, quarter_devices)
    longer = jnp.concatenate([s4, ahead], axis=-3)
    mids = 0.5 * (longer[..., :-1, :, :] + longer[..., 1:, :, :])
    spread = jnp.stack([s4, mids], axis=-3).reshape(
        s4.shape[:-3] + (2 * rows_here,) + s4.shape[-2:]
    )
    spread = rows_up(spread, quarter_devices)
    coarsest_rows = rows_up(spread, sources)

    parts = forward(grids, scal, own_weights, s4)
    s5 = dict(zip(SLOTS, parts[:8]))
    s5_low, s5_high, s5_self = parts[8:11]
    e6 = dict(zip(SLOTS, parts[11:19]))
    d6 = dict(zip(SLOTS, parts[19:27]))
    e6_rest, d6_self = parts[27:]

    from_low = lax.ppermute(s5_low, "dom", [(d, 2 * d) for d in range(sources)])
    from_high = lax.ppermute(s5_high, "dom", [(d, 2 * d + 1) for d in range(sources)])
    c6_rest = e6_rest + from_low + from_high
    firsts = jnp.concatenate(
        [stack_slots({slot: e6[slot][:, :1] for slot in SLOTS}), e6_rest[..., :1, :, :]], axis=3
    )
    e6_ahead = next_row(firsts, dom_size)
    d6_self = d6_self.at[..., -1:, :, :].add(-0.5 * e6_ahead[:, :, :, SHARED_D:])
    d6 = {
        slot: d6[slot].at[:, -1:].add(-0.5 * e6_ahead[slot][:SHARED_D]) for slot in SLOTS
    }

    e6 = {slot: e6[slot].at[:1].add(coarsest_rows[slot]) for slot in SLOTS}

    if square:
        s5_own = reduce_quarter(s5, sources)
        d6_own = reduce_quarter(d6, dom_size)
        e6_own = reduce_quarter(e6, dom_size)
        rest_own = reduce_quarter({slot: c6_rest[slot] for slot in SLOTS}, dom_size)
    else:
        s5_own, e6_own, d6_own, rest_own = lax.psum(
            (stack_slots(s5), stack_slots(e6), stack_slots(d6), c6_rest), ("half", "grid")
        )
    c6_own = e6_own + rows_up(s5_own, sources)
    c5_own = rows_down(c6_own)
    if half_rows > 1:
        pieces = [
            lax.ppermute(
                c6_own[..., :1, ::2, :, :], "dom", [(4 * d + r, d) for d in range(quarter_devices)]
            )
            for r in range(4)
        ]
    else:
        pieces = [
            lax.ppermute(
                c6_own[..., :1, :, :, :], "dom", [(4 * d + r, d) for d in range(quarter_devices)]
            )
            for r in (0, 2)
        ]
    c4_own = jnp.concatenate(pieces, axis=-3)
    c5_own = jnp.concatenate([c5_own, c4_own], axis=-4)
    ahead_own = next_row(
        jnp.concatenate([c6_own[..., :1, :, :], rest_own[..., :1, :, :]], axis=-4), dom_size
    )
    if square:
        d6 = stack_slots(gather_quarters(d6_own, dom_size))
        c6_rest = stack_slots(gather_quarters(rest_own, dom_size))
        c6 = stack_slots(gather_quarters(c6_own, dom_size))
        ahead_row = stack_slots(gather_quarters(ahead_own, dom_size))
        c5 = gather_quarters(c5_own, sources)
    else:
        c6, d6, c6_rest, ahead_row = c6_own, d6_own, rest_own, ahead_own
        c5 = {slot: c5_own[slot] for slot in SLOTS}
    c5_low = lax.ppermute(c6_rest, "dom", [(2 * d, d) for d in range(sources)])
    c5_high = lax.ppermute(c6_rest, "dom", [(2 * d + 1, d) for d in range(sources)])
    values = [c6, c6_rest, ahead_row, d6, d6_self]
    values += [c5, c5_low, c5_high, s5_self]
    return backward(count, scal, rows_here, values)


def solution(mesh):
    return jax.shard_map(
        per_device,
        mesh=mesh,
        in_specs=(P(("half", "grid"), "dom", None, None), P()),
        out_specs=P(("half", "grid"), "dom", None, None),
        check_vma=False,
    )
```

```python
import jax
import jax.numpy as jnp
import numpy as np
from jax import lax
from jax.experimental import pallas as pl
from jax.experimental.pallas import tpu as pltpu
from jax.sharding import PartitionSpec as P


LEV1 = 6
LEV2 = 6
LEV3 = 6
LEV4 = 6
N1 = 64
N2 = 64
N3 = 64
N4 = 64
SPANS = (2, 1, 1, 1)


BLOCKS = (
    (0, 0, 0), (1, 0, 0), (0, 1, 0), (0, 0, 1),
    (1, 1, 0), (1, 0, 1), (0, 1, 1), (1, 1, 1),
)
SHARED_D = 4
SHARED_C = 7
HB = N2 // 2
HC = N3 // 2
HD = N4 // 2
GROUPS = 8
CG = N3 // GROUPS
LANES = HC * HD
HALF_LANES = LANES // 2
QR = HB // 4
TILE = CG // 2 * HD
SLOTS = tuple((h, sx, sy) for h in range(2) for sx in range(2) for sy in range(2))


def combination_weights(levels):
    corners = np.array(
        [[corner >> place & 1 for place in range(4)] for corner in range(16)], dtype=np.int32
    )
    parity = 1 - 2 * (corners.sum(axis=1) % 2)
    raised = levels[:, None, :] + jnp.asarray(corners, dtype=jnp.int32)[None, :, :]
    below = jnp.all(raised[:, :, None, :] <= levels[None, None, :, :], axis=3)
    inside = jnp.any(below, axis=2).astype(jnp.int32)
    return jnp.sum(inside * jnp.asarray(parity, dtype=jnp.int32)[None, :], axis=1)


def split_matrix(count_in, half, wrap):
    table = np.zeros((count_in, 2, half))
    for k in range(half):
        table[2 * k, 0, k] = 1.0
        table[2 * k + 1, 1, k] += 1.0
        table[2 * k, 1, k] -= 0.5
        table[(2 * k + 2) % wrap, 1, k] -= 0.5
    return table


def plain_matrix(count_in, half):
    table = np.zeros((count_in, 1, half))
    for k in range(half):
        table[k, 0, k] = 1.0
    return table


def join_matrix(parts_in, half_out, wrap, next_points):
    table = np.zeros((parts_in, half_out + next_points, 2 * half_out))
    for k in range(half_out):
        table[0, k, 2 * k] = 1.0
        table[1, k, 2 * k + 1] += 1.0
        table[0, k, 2 * k + 1] += 0.5
        table[0, (k + 1) % wrap, 2 * k + 1] += 0.5
    return table


def forward_tables():
    half_c = CG // 2
    tables = {}
    for oc in range(2):
        for od in range(2):
            if oc:
                along_c = split_matrix(CG + 2, half_c, CG + 2)
            else:
                along_c = plain_matrix(half_c, half_c)
            along_d = split_matrix(N4, HD, N4) if od else plain_matrix(N4, HD)
            table = np.einsum("cpk,dql->cdpqkl", along_c, along_d)
            rows = along_c.shape[0] * N4
            tables[oc, od] = jnp.asarray(table.reshape(rows, -1), jnp.bfloat16)
    return tables


def backward_tables():
    half_c = CG // 2
    tables = {}
    for oc in range(2):
        for od in range(2):
            if od:
                along_d = join_matrix(2, HD, HD, 0)
            else:
                along_d = np.zeros((1, HD, N4))
                along_d[0, np.arange(HD), np.arange(HD)] = 1.0
            if oc:
                along_c = join_matrix(2, half_c, half_c + half_c, half_c)
                own = np.einsum("pkc,qld->pqklcd", along_c[:, :half_c], along_d)
                ahead = np.einsum("pkc,qld->pqklcd", along_c[:1, half_c:], along_d)
                cols = CG * N4
                table = np.concatenate([own.reshape(-1, cols), ahead.reshape(-1, cols)], axis=0)
            else:
                along_c = np.eye(half_c)[None]
                table = np.einsum("pkc,qld->pqklcd", along_c, along_d).reshape(-1, half_c * N4)
            tables[oc, od] = jnp.asarray(table, jnp.bfloat16)
    return tables


CASES = ((0, 0), (0, 1), (1, 0), (1, 1))


def split_parts(value):
    high = value.astype(jnp.bfloat16)
    low = (value - high.astype(jnp.float32)).astype(jnp.bfloat16)
    return high, low


def grid_facts(scal, g):
    return tuple(scal[4 * g + axis] for axis in range(4))


def forward_kernel(rows_here, count, scal, fetch, weight, x_ref, *refs):
    tables = dict(zip(CASES, refs[:4]))
    outs = refs[4:-2]
    xb, yb = refs[-2:]
    half_rows = rows_here // 2
    i = pl.program_id(0)
    g = pl.program_id(1)
    level, fine_b, fine_c, fine_d = grid_facts(scal, g)
    mine_x = scal[4 * count]
    mine_y = scal[4 * count + 1]
    row = scal[4 * count + 2] + i
    odd = lax.rem(i, 2) == 1
    even = lax.rem(i, 2) == 0
    active = row < (N1 // 4) * (1 << level)
    active = active & (level > 0)

    def clear(wanted, *targets):
        @pl.when((g == 0) & wanted)
        def _():
            for target in targets:
                target[...] = jnp.zeros_like(target)

    s5 = dict(zip(SLOTS, outs[:8]))
    s5_low, s5_high, s5_self = outs[8:11]
    e6 = dict(zip(SLOTS, outs[11:19]))
    d6 = dict(zip(SLOTS, outs[19:27]))
    e6_rest, d6_self = outs[27:]
    clear(i >= 0, *outs[:8], s5_self)
    clear(i < half_rows, s5_low)
    clear(i >= half_rows, s5_high)
    clear(even, *outs[11:19], e6_rest)
    clear(odd, *outs[19:27], d6_self)

    def put(row_count, fine_c_here):
        rows = slice(0, row_count)
        span = CG * N4 if fine_c_here else CG // 2 * N4
        reach = span + 2 * N4 if fine_c_here else span
        for k in range(GROUPS):
            for lane in range(0, span, 2 * N4):
                value = x_ref[0, 0, rows, k * span + lane : k * span + lane + 2 * N4]
                for place, piece in zip((0, reach), split_parts(value)):
                    xb[k, rows, place + lane : place + lane + 2 * N4] = piece
                    if fine_c_here and lane == 0:
                        before = (k + GROUPS - 1) % GROUPS
                        xb[before, rows, place + span : place + reach] = piece

    for oc, od in CASES:
        for ob in range(2):
            @pl.when(active & (fine_b == ob) & (fine_c == oc) & (fine_d == od))
            def _(oc=oc, od=od, ob=ob):
                rows = (1 + ob) * HB
                put(rows, oc)
                reach = (CG + 2) * N4 if oc else CG // 2 * N4
                table = tables[oc, od][...]
                lhs = xb[:, :rows, : 2 * reach].reshape(GROUPS * rows, 2 * reach)
                result = jnp.dot(
                    lhs[:, :reach], table, preferred_element_type=jnp.float32
                ) + jnp.dot(lhs[:, reach:], table, preferred_element_type=jnp.float32)
                for pc in range(oc + 1):
                    for pd in range(od + 1):
                        column = (pc * (od + 1) + pd) * TILE
                        for k in range(GROUPS):
                            piece = result[k * rows : k * rows + rows, column : column + TILE]
                            if ob:
                                yb[2 * pc + pd, k, :N2] = piece
                                yb[2 * pc + pd, k, N2:] = piece[:QR]
                            else:
                                yb[2 * pc + pd, k, pl.ds(0, HB, stride=2)] = piece

    scale = weight[g]

    def add_up(wanted, blocks, target):
        for block in blocks:
            pb, pc, pd = BLOCKS[block]

            @pl.when(wanted & (pb <= fine_b) & (pc <= fine_c) & (pd <= fine_d))
            def _(block=block, pb=pb, part=2 * pc + pd):
                for h, sx, sy in SLOTS:
                    quarter = 2 * (sx ^ mine_x) + (sy ^ mine_y)
                    start = pl.multiple_of(quarter * 2 * QR, 2 * QR)
                    ref, index = target(block, h, sx, sy)
                    for j in range(GROUPS // 2):
                        k = h * (GROUPS // 2) + j
                        piece = yb[part, k, pl.ds(start, QR, stride=2)]
                        if pb:
                            piece = yb[part, k, pl.ds(start + 1, QR, stride=2)] - 0.5 * (
                                piece + yb[part, k, pl.ds(start + 2, QR, stride=2)]
                            )
                        where = index + (slice(None), slice(j * TILE, j * TILE + TILE))
                        ref[where] += scale * piece

    def slot_of(parts):
        return lambda block, h, sx, sy: (parts[h, sx, sy], (block, 0))

    def rest_of(ref):
        return lambda block, h, sx, sy: (ref, (h, sx, sy, block - SHARED_D, 0))

    def line_of(ref):
        return lambda block, h, sx, sy: (ref, (h, sx, sy, 0))

    six = active & (level == 2)
    five = active & (level == 1)
    add_up(six & even, range(SHARED_D), slot_of(e6))
    add_up(six & even, range(SHARED_D, SHARED_C), rest_of(e6_rest))
    add_up(six & odd, range(SHARED_D), slot_of(d6))
    add_up(six & odd, range(SHARED_D, SHARED_C), rest_of(d6_self))
    add_up(five, range(SHARED_D), slot_of(s5))
    add_up(five & (i < half_rows), range(SHARED_D, SHARED_C), rest_of(s5_low))
    add_up(five & (i >= half_rows), range(SHARED_D, SHARED_C), rest_of(s5_high))
    add_up(five, range(SHARED_C, 8), line_of(s5_self))

    @pl.when((g == count - 1) & (i > 0))
    def _():
        for slot in SLOTS:
            d6[slot][...] -= 0.5 * e6[slot][...]
        d6_self[...] -= 0.5 * e6_rest[...]


def forward(grids, scal, weight):
    count, rows_here = grids.shape[:2]
    half_rows = rows_here // 2
    tables = forward_tables()
    levels = scal[: 4 * count].reshape(count, 4)[:, 0]
    rows = scal[4 * count + 2] + jnp.arange(rows_here, dtype=jnp.int32)
    takes = (levels > 0)[None, :] & (rows[:, None] < (N1 // 4) * (1 << levels)[None, :])
    steps = jnp.arange(rows_here * count, dtype=jnp.int32)
    earlier = (steps[None, :] <= steps[:, None]) & takes.reshape(-1)[None, :]
    fetch = jnp.max(jnp.where(earlier, steps[None, :], 0), axis=1)

    def constant(table):
        return pl.BlockSpec(table.shape, lambda i, g, *_: (0, 0))

    def page(i, g, scal, fetch, weight):
        step = fetch[i * count + g]
        return (lax.rem(step, count), step // count, 0, 0)

    def rows_spec(blocks, row_of):
        return pl.BlockSpec(
            (blocks, 1, QR, HALF_LANES), lambda i, g, *_: (0, row_of(i), 0, 0)
        )

    def shape(*dims):
        return jax.ShapeDtypeStruct(dims + (QR, HALF_LANES), jnp.float32)

    def even_row(i):
        return i // 2

    def odd_row(i):
        return jnp.maximum(i - 1, 0) // 2

    rest = SHARED_C - SHARED_D
    out_specs = (
        [rows_spec(SHARED_D, lambda i: i)] * 8
        + [
            rest_spec(rest, lambda i: jnp.minimum(i, half_rows - 1)),
            rest_spec(rest, lambda i: jnp.maximum(i - half_rows, 0)),
            line_spec(lambda i: i),
        ]
        + [rows_spec(SHARED_D, even_row)] * 8
        + [rows_spec(SHARED_D, odd_row)] * 8
        + [rest_spec(rest, even_row), rest_spec(rest, odd_row)]
    )
    out_shape = (
        [shape(SHARED_D, rows_here)] * 8
        + [shape(2, 2, 2, rest, half_rows)] * 2
        + [shape(2, 2, 2, rows_here)]
        + [shape(SHARED_D, half_rows)] * 16
        + [shape(2, 2, 2, rest, half_rows)] * 2
    )
    ordered = [tables[case] for case in CASES]
    return pl.pallas_call(
        lambda *refs: forward_kernel(rows_here, count, *refs),
        grid_spec=pltpu.PrefetchScalarGridSpec(
            num_scalar_prefetch=3,
            grid=(rows_here, count),
            in_specs=[pl.BlockSpec((1, 1, N2, N3 * N4), page)]
            + [constant(table) for table in ordered],
            out_specs=out_specs,
            scratch_shapes=[
                pltpu.VMEM((GROUPS, 2 * HB, 2 * (CG + 2) * N4), jnp.bfloat16),
                pltpu.VMEM((4, GROUPS, N2 + QR, TILE), jnp.float32),
            ],
        ),
        out_shape=out_shape,
        compiler_params=pltpu.CompilerParams(vmem_limit_bytes=60 * 2**20),
        cost_estimate=pl.CostEstimate(
            flops=10**10, bytes_accessed=60 * 2**20, transcendentals=0
        ),
        name="split_grids",
    )(scal, fetch, weight, grids, *ordered)


def coarsest_kernel(count, scal, weight, x_ref, table, after, out, yb):
    i = pl.program_id(0)
    mine_x = scal[4 * count]
    mine_y = scal[4 * count + 1]
    g = scal[4 * count + 3]
    active = (scal[4 * g] == 0) & (scal[4 * count + 2] + i < N1 // 4)

    @pl.when(jnp.logical_not(active))
    def _():
        out[...] = jnp.zeros_like(out)

    @pl.when(active)
    def _():
        span = CG // 2 * N4
        for k in range(GROUPS):
            high, low = split_parts(x_ref[0, 0, :, k * span : k * span + span])
            yb[k] = weight[g] * (
                jnp.dot(high, table[...], preferred_element_type=jnp.float32)
                + jnp.dot(low, table[...], preferred_element_type=jnp.float32)
            )
        for h, sx, sy in SLOTS:
            quarter = 2 * (sx ^ mine_x) + (sy ^ mine_y)
            start = pl.multiple_of(quarter * QR, QR)
            for j in range(GROUPS // 2):
                out[h, sx, sy, 0, :, j * TILE : j * TILE + TILE] = yb[
                    h * (GROUPS // 2) + j, pl.ds(start, QR)
                ]


def coarsest(grids, scal, weight, after):
    count, rows_here = grids.shape[:2]
    table = forward_tables()[0, 0]

    def page(i, scal, weight):
        g = scal[4 * count + 3]
        wanted = (scal[4 * g] == 0) & (scal[4 * count + 2] + i < N1 // 4)
        return (g, jnp.where(wanted, i, 0), 0, 0)

    return pl.pallas_call(
        lambda *refs: coarsest_kernel(count, *refs),
        grid_spec=pltpu.PrefetchScalarGridSpec(
            num_scalar_prefetch=2,
            grid=(rows_here,),
            in_specs=[
                pl.BlockSpec((1, 1, HB, HC * N4), page),
                pl.BlockSpec(table.shape, lambda i, *_: (0, 0)),
                pl.BlockSpec(memory_space=pl.ANY),
            ],
            out_specs=line_spec(lambda i: i),
            scratch_shapes=[pltpu.VMEM((GROUPS, HB, TILE), jnp.float32)],
        ),
        out_shape=jax.ShapeDtypeStruct((2, 2, 2, rows_here, QR, HALF_LANES), jnp.float32),
        compiler_params=pltpu.CompilerParams(vmem_limit_bytes=60 * 2**20),
        cost_estimate=pl.CostEstimate(
            flops=10**8, bytes_accessed=4 * 2**20, transcendentals=0
        ),
        name="split_coarsest",
    )(scal, weight, grids, table, after)


def rest_spec(blocks, row_of):
    return pl.BlockSpec(
        (2, 2, 2, blocks, 1, QR, HALF_LANES), lambda i, g, *_: (0, 0, 0, 0, row_of(i), 0, 0)
    )


def line_spec(row_of):
    return pl.BlockSpec(
        (2, 2, 2, 1, QR, HALF_LANES), lambda i, *_: (0, 0, 0, row_of(i), 0, 0)
    )


def backward_kernel(rows_here, count, scal, *refs):
    used = 19
    c6, c6_next, c6_rest, c6_rest_next, ahead_row, d6, d6_self = refs[:7]
    c5 = dict(zip(SLOTS, refs[7:15]))
    c5_low, c5_high, s5_self, c4 = refs[15:19]
    tables = dict(zip(CASES, refs[used : used + 4]))
    out = refs[used + 4]
    coarse, detail, joined, xb = refs[used + 5 :]
    half_rows = rows_here // 2
    i = pl.program_id(0)
    g = pl.program_id(1)
    level, fine_b, fine_c, fine_d = grid_facts(scal, g)
    mine_x = scal[4 * count]
    mine_y = scal[4 * count + 1]
    row = scal[4 * count + 2] + i
    odd = lax.rem(i, 2) == 1
    even = lax.rem(i, 2) == 0
    active = row < (N1 // 4) * (1 << level)

    def stage(wanted, blocks, source):
        for block in blocks:
            pb, pc, pd = BLOCKS[block]

            @pl.when(active & wanted & (pb <= fine_b) & (pc <= fine_c) & (pd <= fine_d))
            def _(block=block, work=(coarse, detail)[pb], part=2 * pc + pd):
                for h, sx, sy in SLOTS:
                    quarter = 2 * (sx ^ mine_x) + (sy ^ mine_y)
                    start = pl.multiple_of(quarter * QR, QR)
                    value = source(block, h, sx, sy)
                    for j in range(GROUPS // 2):
                        k = h * (GROUPS // 2) + j
                        work[part, k, pl.ds(start, QR)] = value[:, j * TILE : j * TILE + TILE]

    def here(block, h, sx, sy):
        if block < SHARED_D:
            return c6[h, sx, sy, block, 0]
        return c6_rest[h, sx, sy, block - SHARED_D, 0]

    def between(last):
        def value(block, h, sx, sy):
            if last:
                after = ahead_row[h, sx, sy, block, 0]
            elif block < SHARED_D:
                after = c6_next[h, sx, sy, block, 0]
            else:
                after = c6_rest_next[h, sx, sy, block - SHARED_D, 0]
            mean = 0.5 * (here(block, h, sx, sy) + after)
            if block < SHARED_D:
                return mean + d6[h, sx, sy, block, 0]
            return mean + d6_self[h, sx, sy, block - SHARED_D, 0]

        return value

    stage((level == 2) & even, range(SHARED_C), here)
    if half_rows > 1:
        stage((level == 2) & odd & (i < rows_here - 1), range(SHARED_C), between(False))
    stage((level == 2) & odd & (i == rows_here - 1), range(SHARED_C), between(True))
    rest = range(SHARED_D, SHARED_C)
    five = level == 1
    stage(five, range(SHARED_D), lambda b, h, x, y: c5[h, x, y][b, 0])
    stage(five & (i < half_rows), rest, lambda b, h, x, y: c5_low[h, x, y, b - SHARED_D, 0])
    stage(five & (i >= half_rows), rest, lambda b, h, x, y: c5_high[h, x, y, b - SHARED_D, 0])
    stage(five, range(SHARED_C, 8), lambda b, h, x, y: s5_self[h, x, y, 0])
    stage(level == 0, range(1), lambda b, h, x, y: c4[h, x, y, 0])

    @pl.when(jnp.logical_not(active))
    def _():
        out[...] = jnp.zeros_like(out)

    for oc, od in CASES:
        for ob in range(2):
            @pl.when(active & (fine_b == ob) & (fine_c == oc) & (fine_d == od))
            def _(oc=oc, od=od, ob=ob):
                parts = [(pc, pd) for pc in range(oc + 1) for pd in range(od + 1)]
                ahead = [(0, pd) for pd in range(od + 1)] if oc else []
                reach = (len(parts) + len(ahead)) * TILE
                rows = (1 + ob) * HB
                for place, (pc, pd) in enumerate(parts):
                    part = 2 * pc + pd
                    for k in range(GROUPS):
                        value = coarse[part, k, :HB]
                        if ob:
                            coarse[part, k, HB:] = coarse[part, k, :QR]
                            mean = 0.5 * (value + coarse[part, k, 1 : HB + 1])
                            joined[k, pl.ds(0, HB, stride=2)] = value
                            joined[k, pl.ds(1, HB, stride=2)] = detail[part, k] + mean
                            value = joined[k]
                        for base, piece in zip((0, reach), split_parts(value)):
                            start = base + place * TILE
                            xb[k, :rows, start : start + TILE] = piece
                            if oc and not pc:
                                start = base + (len(parts) + pd) * TILE
                                before = (k + GROUPS - 1) % GROUPS
                                xb[before, :rows, start : start + TILE] = piece
                table = tables[oc, od][...]
                lhs = xb[:, :rows, : 2 * reach].reshape(GROUPS * rows, 2 * reach)
                result = jnp.dot(
                    lhs[:, :reach], table, preferred_element_type=jnp.float32
                ) + jnp.dot(lhs[:, reach:], table, preferred_element_type=jnp.float32)
                span = CG * N4 if oc else CG // 2 * N4
                for k in range(GROUPS):
                    out[0, 0, :rows, k * span : k * span + span] = result[
                        k * rows : k * rows + rows
                    ]
                if not ob:
                    out[0, 0, HB:, :] = jnp.zeros((HB, N3 * N4), jnp.float32)
                if not oc:
                    out[0, 0, :, HC * N4 :] = jnp.zeros((N2, HC * N4), jnp.float32)


def backward(count, scal, rows_here, values):
    half_rows = rows_here // 2
    tables = backward_tables()
    ordered = [tables[case] for case in CASES]

    def constant(table):
        return pl.BlockSpec(table.shape, lambda i, g, *_: (0, 0))

    rest = SHARED_C - SHARED_D
    c6, c6_rest, ahead_row, d6, d6_self = values[:5]
    operands = [c6, c6, c6_rest, c6_rest, ahead_row, d6, d6_self]
    following = lambda i: jnp.minimum((i + 1) // 2, half_rows - 1)
    in_specs = [
        rest_spec(SHARED_D, lambda i: i // 2),
        rest_spec(SHARED_D, following),
        rest_spec(rest, lambda i: i // 2),
        rest_spec(rest, following),
        rest_spec(SHARED_C, lambda i: 0),
        rest_spec(SHARED_D, lambda i: i // 2),
        rest_spec(rest, lambda i: i // 2),
    ]
    c5, c5_low, c5_high, s5_self = values[5:]
    operands += [c5[slot] for slot in SLOTS] + [c5_low, c5_high, s5_self]
    in_specs += [
        pl.BlockSpec((SHARED_D, 1, QR, HALF_LANES), lambda i, g, *_: (0, i, 0, 0))
    ] * 8 + [
        rest_spec(rest, lambda i: jnp.minimum(i, half_rows - 1)),
        rest_spec(rest, lambda i: jnp.maximum(i - half_rows, 0)),
        line_spec(lambda i: i),
    ]
    c4 = jnp.stack([c5[slot][SHARED_D] for slot in SLOTS])
    operands.append(c4.reshape((2, 2, 2) + c4.shape[1:]))
    in_specs.append(line_spec(lambda i: i))
    return pl.pallas_call(
        lambda *refs: backward_kernel(rows_here, count, *refs),
        grid_spec=pltpu.PrefetchScalarGridSpec(
            num_scalar_prefetch=1,
            grid=(rows_here, count),
            in_specs=in_specs + [constant(table) for table in ordered],
            out_specs=pl.BlockSpec((1, 1, N2, N3 * N4), lambda i, g, *_: (g, i, 0, 0)),
            scratch_shapes=[
                pltpu.VMEM((4, GROUPS, HB + QR, TILE), jnp.float32),
                pltpu.VMEM((4, GROUPS, HB, TILE), jnp.float32),
                pltpu.VMEM((GROUPS, N2, TILE), jnp.float32),
                pltpu.VMEM((GROUPS, N2, 12 * TILE), jnp.bfloat16),
            ],
        ),
        out_shape=jax.ShapeDtypeStruct((count, rows_here, N2, N3 * N4), jnp.float32),
        compiler_params=pltpu.CompilerParams(vmem_limit_bytes=60 * 2**20),
        cost_estimate=pl.CostEstimate(
            flops=10**10, bytes_accessed=60 * 2**20, transcendentals=0
        ),
        name="join_grids",
    )(scal, *operands, *ordered)


def stack_slots(pieces):
    return jnp.stack(
        [
            jnp.stack([jnp.stack([pieces[h, sx, sy] for sy in range(2)]) for sx in range(2)])
            for h in range(2)
        ]
    )


def exchange(value, axis, domains):
    dom_count = lax.axis_size("dom")
    pairs = []
    for x in range(2):
        for y in range(2):
            other = (1 - x, y) if axis == "half" else (x, 1 - y)
            for d in range(domains):
                pairs.append(
                    ((x * 2 + y) * dom_count + d, (other[0] * 2 + other[1]) * dom_count + d)
                )
    return lax.ppermute(value, ("half", "grid", "dom"), pairs)


def reduce_quarter(pieces, domains):
    reduced = []
    for h in range(2):
        first, second = (("half", "grid"), ("grid", "half"))[h]
        far = lambda a, b: pieces[(h, a, b) if h == 0 else (h, b, a)]
        onward = exchange(far(1, 1), first, domains)
        nearby = exchange(far(1, 0), first, domains)
        onward = far(0, 1) + onward
        nearby = far(0, 0) + nearby
        onward = exchange(onward, second, domains)
        reduced.append(nearby + onward)
    return jnp.stack(reduced)


def gather_quarters(own, domains):
    pieces = {}
    for h in range(2):
        first, second = (("half", "grid"), ("grid", "half"))[h]
        place = lambda a, b: (h, a, b) if h == 0 else (h, b, a)
        pieces[place(0, 0)] = own[h]
        pieces[place(0, 1)] = exchange(own[h], second, domains)
        pieces[place(1, 0)] = exchange(own[h], first, domains)
        pieces[place(1, 1)] = exchange(pieces[place(0, 1)], first, domains)
    return pieces


def rows_up(value, sources):
    half_rows = value.shape[-3] // 2
    low = lax.ppermute(value[..., :half_rows, :, :], "dom", [(d, 2 * d) for d in range(sources)])
    high = lax.ppermute(
        value[..., half_rows:, :, :], "dom", [(d, 2 * d + 1) for d in range(sources)]
    )
    return low + high


def rows_down(value):
    targets = lax.axis_size("dom") // 2
    low = lax.ppermute(value, "dom", [(2 * d, d) for d in range(targets)])
    high = lax.ppermute(value, "dom", [(2 * d + 1, d) for d in range(targets)])
    return jnp.concatenate([low, high], axis=-3)


def next_row(value, devices):
    return lax.ppermute(
        value[..., :1, :, :], "dom", [((d + 1) % devices, d) for d in range(devices)]
    )


def per_device(grids, levels):
    count, rows_here = grids.shape[:2]
    half_rows = rows_here // 2
    half_size = lax.axis_size("half")
    grid_size = lax.axis_size("grid")
    dom_size = lax.axis_size("dom")
    square = half_size == 2 and grid_size == 2
    group = lax.axis_index("half") * grid_size + lax.axis_index("grid")
    weights = combination_weights(levels).astype(jnp.float32)
    lowest = jnp.array(
        [LEV1 - SPANS[0], LEV2 - SPANS[1], LEV3 - SPANS[2], LEV4 - SPANS[3]], dtype=jnp.int32
    )
    offsets = levels - lowest[None, :]
    own_offsets = lax.dynamic_slice_in_dim(offsets, group * count, count, 0)
    own_weights = lax.dynamic_slice_in_dim(weights, group * count, count, 0)
    zero = jnp.zeros((), jnp.int32)
    place = jnp.stack(
        [
            lax.axis_index("half") if square else zero,
            lax.axis_index("grid") if square else zero,
            lax.axis_index("dom") * rows_here,
        ]
    ).astype(jnp.int32)
    first = jnp.argmax(own_offsets[:, 0] == 0).astype(jnp.int32)
    scal = jnp.concatenate([own_offsets.reshape(-1), place, first[None]])
    sources = dom_size // 2
    quarter_devices = dom_size // 4
    parts = forward(grids, scal, own_weights)
    s5 = dict(zip(SLOTS, parts[:8]))
    s5_low, s5_high, s5_self = parts[8:11]
    e6 = dict(zip(SLOTS, parts[11:19]))
    d6 = dict(zip(SLOTS, parts[19:27]))
    e6_rest, d6_self = parts[27:]

    from_low = lax.ppermute(s5_low, "dom", [(d, 2 * d) for d in range(sources)])
    from_high = lax.ppermute(s5_high, "dom", [(d, 2 * d + 1) for d in range(sources)])
    c6_rest = e6_rest + from_low + from_high
    firsts = jnp.concatenate(
        [stack_slots({slot: e6[slot][:, :1] for slot in SLOTS}), e6_rest[..., :1, :, :]], axis=3
    )
    e6_ahead = next_row(firsts, dom_size)
    d6_self = d6_self.at[..., -1:, :, :].add(-0.5 * e6_ahead[:, :, :, SHARED_D:])
    d6 = {
        slot: d6[slot].at[:, -1:].add(-0.5 * e6_ahead[slot][:SHARED_D]) for slot in SLOTS
    }

    s4 = coarsest(grids, scal, own_weights, s5_self)
    taken = max(half_rows // 2, 1) + 1
    lines = 0.0
    for r in range(4):
        start = half_rows * r // 2
        sent = s4[:, :, :, start : start + taken]
        if sent.shape[3] < taken:
            sent = jnp.pad(sent, ((0, 0),) * 3 + ((0, taken - sent.shape[3]),) + ((0, 0),) * 2)
        pairs = [(d, 4 * d + r) for d in range(quarter_devices)]
        lines = lines + lax.ppermute(sent, "dom", pairs)
    tops = tuple(r for r in range(4) if half_rows * r // 2 + taken > rows_here)
    for r in tops:
        pairs = [((d + 1) % quarter_devices, 4 * d + r) for d in range(quarter_devices)]
        lines = lines.at[:, :, :, -1:].add(lax.ppermute(s4[:, :, :, :1], "dom", pairs))
    means = 0.5 * (lines[:, :, :, :-1] + lines[:, :, :, 1:])
    lines = lines[:, :, :, :-1]
    if half_rows > 1:
        coarsest_rows = jnp.stack([lines, means], axis=4).reshape(
            (2, 2, 2, 1, half_rows) + lines.shape[-2:]
        )
    else:
        between_rows = lax.rem(lax.axis_index("dom"), 2) == 1
        coarsest_rows = jnp.where(between_rows, means, lines)[:, :, :, None]
    e6 = {slot: e6[slot].at[:1].add(coarsest_rows[slot]) for slot in SLOTS}

    if square:
        s5_own = reduce_quarter(s5, sources)
        d6_own = reduce_quarter(d6, dom_size)
        e6_own = reduce_quarter(e6, dom_size)
        rest_own = reduce_quarter({slot: c6_rest[slot] for slot in SLOTS}, dom_size)
    else:
        s5_own, e6_own, d6_own, rest_own = lax.psum(
            (stack_slots(s5), stack_slots(e6), stack_slots(d6), c6_rest), ("half", "grid")
        )
    c6_own = e6_own + rows_up(s5_own, sources)
    c5_own = rows_down(c6_own)
    if half_rows > 1:
        pieces = [
            lax.ppermute(
                c6_own[..., :1, ::2, :, :], "dom", [(4 * d + r, d) for d in range(quarter_devices)]
            )
            for r in range(4)
        ]
    else:
        pieces = [
            lax.ppermute(
                c6_own[..., :1, :, :, :], "dom", [(4 * d + r, d) for d in range(quarter_devices)]
            )
            for r in (0, 2)
        ]
    c4_own = jnp.concatenate(pieces, axis=-3)
    c5_own = jnp.concatenate([c5_own, c4_own], axis=-4)
    ahead_own = next_row(
        jnp.concatenate([c6_own[..., :1, :, :], rest_own[..., :1, :, :]], axis=-4), dom_size
    )
    if square:
        d6 = stack_slots(gather_quarters(d6_own, dom_size))
        c6_rest = stack_slots(gather_quarters(rest_own, dom_size))
        c6 = stack_slots(gather_quarters(c6_own, dom_size))
        ahead_row = stack_slots(gather_quarters(ahead_own, dom_size))
        c5 = gather_quarters(c5_own, sources)
    else:
        c6, d6, c6_rest, ahead_row = c6_own, d6_own, rest_own, ahead_own
        c5 = {slot: c5_own[slot] for slot in SLOTS}
    c5_low = lax.ppermute(c6_rest, "dom", [(2 * d, d) for d in range(sources)])
    c5_high = lax.ppermute(c6_rest, "dom", [(2 * d + 1, d) for d in range(sources)])
    values = [c6, c6_rest, ahead_row, d6, d6_self]
    values += [c5, c5_low, c5_high, s5_self]
    return backward(count, scal, rows_here, values)


def solution(mesh):
    return jax.shard_map(
        per_device,
        mesh=mesh,
        in_specs=(P(("half", "grid"), "dom", None, None), P()),
        out_specs=P(("half", "grid"), "dom", None, None),
        check_vma=False,
    )
```

```python
import jax
import jax.numpy as jnp
import numpy as np
from jax import lax
from jax.experimental import pallas as pl
from jax.experimental.pallas import tpu as pltpu
from jax.sharding import PartitionSpec as P


LEV1 = 6
LEV2 = 6
LEV3 = 6
LEV4 = 6
N1 = 64
N2 = 64
N3 = 64
N4 = 64
SPANS = (2, 1, 1, 1)


BLOCKS = (
    (0, 0, 0), (1, 0, 0), (0, 1, 0), (0, 0, 1),
    (1, 1, 0), (1, 0, 1), (0, 1, 1), (1, 1, 1),
)
SHARED_D = 4
SHARED_C = 7
HB = N2 // 2
HC = N3 // 2
HD = N4 // 2
GROUPS = 8
CG = N3 // GROUPS
LANES = HC * HD
HALF_LANES = LANES // 2
QR = HB // 4
TILE = CG // 2 * HD
SLOTS = tuple((h, sx, sy) for h in range(2) for sx in range(2) for sy in range(2))


def combination_weights(levels):
    corners = np.array(
        [[corner >> place & 1 for place in range(4)] for corner in range(16)], dtype=np.int32
    )
    parity = 1 - 2 * (corners.sum(axis=1) % 2)
    raised = levels[:, None, :] + jnp.asarray(corners, dtype=jnp.int32)[None, :, :]
    below = jnp.all(raised[:, :, None, :] <= levels[None, None, :, :], axis=3)
    inside = jnp.any(below, axis=2).astype(jnp.int32)
    return jnp.sum(inside * jnp.asarray(parity, dtype=jnp.int32)[None, :], axis=1)


def split_matrix(count_in, half, wrap):
    table = np.zeros((count_in, 2, half))
    for k in range(half):
        table[2 * k, 0, k] = 1.0
        table[2 * k + 1, 1, k] += 1.0
        table[2 * k, 1, k] -= 0.5
        table[(2 * k + 2) % wrap, 1, k] -= 0.5
    return table


def plain_matrix(count_in, half):
    table = np.zeros((count_in, 1, half))
    for k in range(half):
        table[k, 0, k] = 1.0
    return table


def join_matrix(parts_in, half_out, wrap, next_points):
    table = np.zeros((parts_in, half_out + next_points, 2 * half_out))
    for k in range(half_out):
        table[0, k, 2 * k] = 1.0
        table[1, k, 2 * k + 1] += 1.0
        table[0, k, 2 * k + 1] += 0.5
        table[0, (k + 1) % wrap, 2 * k + 1] += 0.5
    return table


def forward_tables():
    half_c = CG // 2
    tables = {}
    for oc in range(2):
        for od in range(2):
            if oc:
                along_c = split_matrix(CG + 2, half_c, CG + 2)
            else:
                along_c = plain_matrix(half_c, half_c)
            along_d = split_matrix(N4, HD, N4) if od else plain_matrix(N4, HD)
            table = np.einsum("cpk,dql->cdpqkl", along_c, along_d)
            rows = along_c.shape[0] * N4
            tables[oc, od] = jnp.asarray(table.reshape(rows, -1), jnp.bfloat16)
    return tables


def backward_tables():
    half_c = CG // 2
    tables = {}
    for oc in range(2):
        for od in range(2):
            if od:
                along_d = join_matrix(2, HD, HD, 0)
            else:
                along_d = np.zeros((1, HD, N4))
                along_d[0, np.arange(HD), np.arange(HD)] = 1.0
            if oc:
                along_c = join_matrix(2, half_c, half_c + half_c, half_c)
                own = np.einsum("pkc,qld->pqklcd", along_c[:, :half_c], along_d)
                ahead = np.einsum("pkc,qld->pqklcd", along_c[:1, half_c:], along_d)
                cols = CG * N4
                table = np.concatenate([own.reshape(-1, cols), ahead.reshape(-1, cols)], axis=0)
            else:
                along_c = np.eye(half_c)[None]
                table = np.einsum("pkc,qld->pqklcd", along_c, along_d).reshape(-1, half_c * N4)
            tables[oc, od] = jnp.asarray(table, jnp.bfloat16)
    return tables


CASES = ((0, 0), (0, 1), (1, 0), (1, 1))


def split_parts(value):
    high = value.astype(jnp.bfloat16)
    low = (value - high.astype(jnp.float32)).astype(jnp.bfloat16)
    return high, low


def grid_facts(scal, g):
    return tuple(scal[4 * g + axis] for axis in range(4))


def forward_kernel(rows_here, count, scal, weight, x_ref, *refs):
    tables = dict(zip(CASES, refs[:4]))
    outs = refs[4:-2]
    xb, yb = refs[-2:]
    half_rows = rows_here // 2
    i = pl.program_id(0)
    mine_x = scal[4 * count]
    mine_y = scal[4 * count + 1]
    row = scal[4 * count + 2] + i
    odd = lax.rem(i, 2) == 1
    even = lax.rem(i, 2) == 0

    def clear(wanted, *targets):
        @pl.when(wanted)
        def _():
            for target in targets:
                target[...] = jnp.zeros_like(target)

    s5 = dict(zip(SLOTS, outs[:8]))
    s5_low, s5_high, s5_self = outs[8:11]
    e6 = dict(zip(SLOTS, outs[11:19]))
    d6 = dict(zip(SLOTS, outs[19:27]))
    e6_rest, d6_self = outs[27:]
    clear(i >= 0, *outs[:8], s5_self)
    clear(i < half_rows, s5_low)
    clear(i >= half_rows, s5_high)
    clear(even, *outs[11:19], e6_rest)
    clear(odd, *outs[19:27], d6_self)

    def one_grid(g, carry):
        level, fine_b, fine_c, fine_d = grid_facts(scal, g)
        active = row < (N1 // 4) * (1 << level)

        def put(row_count, fine_c_here):
            rows = slice(0, row_count)
            span = CG * N4 if fine_c_here else CG // 2 * N4
            reach = span + 2 * N4 if fine_c_here else span
            for k in range(GROUPS):
                for lane in range(0, span, 2 * N4):
                    value = x_ref[g, 0, rows, k * span + lane : k * span + lane + 2 * N4]
                    for place, piece in zip((0, reach), split_parts(value)):
                        xb[k, rows, place + lane : place + lane + 2 * N4] = piece
                        if fine_c_here and lane == 0:
                            before = (k + GROUPS - 1) % GROUPS
                            xb[before, rows, place + span : place + reach] = piece

        for oc, od in CASES:
            for ob in range(2):
                @pl.when(active & (fine_b == ob) & (fine_c == oc) & (fine_d == od))
                def _(oc=oc, od=od, ob=ob):
                    rows = (1 + ob) * HB
                    put(rows, oc)
                    reach = (CG + 2) * N4 if oc else CG // 2 * N4
                    table = tables[oc, od][...]
                    lhs = xb[:, :rows, : 2 * reach].reshape(GROUPS * rows, 2 * reach)
                    result = jnp.dot(
                        lhs[:, :reach], table, preferred_element_type=jnp.float32
                    ) + jnp.dot(lhs[:, reach:], table, preferred_element_type=jnp.float32)
                    for pc in range(oc + 1):
                        for pd in range(od + 1):
                            column = (pc * (od + 1) + pd) * TILE
                            for k in range(GROUPS):
                                piece = result[k * rows : k * rows + rows, column : column + TILE]
                                if ob:
                                    yb[2 * pc + pd, k, :N2] = piece
                                    yb[2 * pc + pd, k, N2:] = piece[:QR]
                                else:
                                    yb[2 * pc + pd, k, pl.ds(0, HB, stride=2)] = piece

        scale = weight[g]

        def add_up(wanted, blocks, target):
            for block in blocks:
                pb, pc, pd = BLOCKS[block]

                @pl.when(wanted & (pb <= fine_b) & (pc <= fine_c) & (pd <= fine_d))
                def _(block=block, pb=pb, part=2 * pc + pd):
                    for h, sx, sy in SLOTS:
                        quarter = 2 * (sx ^ mine_x) + (sy ^ mine_y)
                        start = pl.multiple_of(quarter * 2 * QR, 2 * QR)
                        ref, index = target(block, h, sx, sy)
                        for j in range(GROUPS // 2):
                            k = h * (GROUPS // 2) + j
                            piece = yb[part, k, pl.ds(start, QR, stride=2)]
                            if pb:
                                piece = yb[part, k, pl.ds(start + 1, QR, stride=2)] - 0.5 * (
                                    piece + yb[part, k, pl.ds(start + 2, QR, stride=2)]
                                )
                            where = index + (slice(None), slice(j * TILE, j * TILE + TILE))
                            ref[where] += scale * piece

        def slot_of(parts):
            return lambda block, h, sx, sy: (parts[h, sx, sy], (block, 0))

        def rest_of(ref):
            return lambda block, h, sx, sy: (ref, (h, sx, sy, block - SHARED_D, 0))

        def line_of(ref):
            return lambda block, h, sx, sy: (ref, (h, sx, sy, 0))

        six = active & (level == 2)
        five = active & (level == 1)
        add_up(six & even, range(SHARED_D), slot_of(e6))
        add_up(six & even, range(SHARED_D, SHARED_C), rest_of(e6_rest))
        add_up(six & odd, range(SHARED_D), slot_of(d6))
        add_up(six & odd, range(SHARED_D, SHARED_C), rest_of(d6_self))
        add_up(five, range(SHARED_D), slot_of(s5))
        add_up(five & (i < half_rows), range(SHARED_D, SHARED_C), rest_of(s5_low))
        add_up(five & (i >= half_rows), range(SHARED_D, SHARED_C), rest_of(s5_high))
        add_up(five, range(SHARED_C, 8), line_of(s5_self))
        add_up(
            active & (level == 0),
            range(1),
            lambda block, h, sx, sy: (s5[h, sx, sy], (SHARED_D, 0)),
        )
        return carry

    lax.fori_loop(0, count, one_grid, 0)

    @pl.when(i > 0)
    def _():
        for slot in SLOTS:
            d6[slot][...] -= 0.5 * e6[slot][...]
        d6_self[...] -= 0.5 * e6_rest[...]


def forward(grids, scal, weight):
    count, rows_here = grids.shape[:2]
    half_rows = rows_here // 2
    tables = forward_tables()

    def constant(table):
        return pl.BlockSpec(table.shape, lambda i, *_: (0, 0))

    def rows_spec(blocks, row_of):
        return pl.BlockSpec(
            (blocks, 1, QR, HALF_LANES), lambda i, *_: (0, row_of(i), 0, 0)
        )

    def shape(*dims):
        return jax.ShapeDtypeStruct(dims + (QR, HALF_LANES), jnp.float32)

    def even_row(i):
        return i // 2

    def odd_row(i):
        return jnp.maximum(i - 1, 0) // 2

    rest = SHARED_C - SHARED_D
    out_specs = (
        [rows_spec(SHARED_D + 1, lambda i: i)] * 8
        + [
            rest_spec(rest, lambda i: jnp.minimum(i, half_rows - 1)),
            rest_spec(rest, lambda i: jnp.maximum(i - half_rows, 0)),
            line_spec(lambda i: i),
        ]
        + [rows_spec(SHARED_D, even_row)] * 8
        + [rows_spec(SHARED_D, odd_row)] * 8
        + [rest_spec(rest, even_row), rest_spec(rest, odd_row)]
    )
    out_shape = (
        [shape(SHARED_D + 1, rows_here)] * 8
        + [shape(2, 2, 2, rest, half_rows)] * 2
        + [shape(2, 2, 2, rows_here)]
        + [shape(SHARED_D, half_rows)] * 16
        + [shape(2, 2, 2, rest, half_rows)] * 2
    )
    ordered = [tables[case] for case in CASES]
    return pl.pallas_call(
        lambda *refs: forward_kernel(rows_here, count, *refs),
        grid_spec=pltpu.PrefetchScalarGridSpec(
            num_scalar_prefetch=2,
            grid=(rows_here,),
            in_specs=[pl.BlockSpec((count, 1, N2, N3 * N4), lambda i, *_: (0, i, 0, 0))]
            + [constant(table) for table in ordered],
            out_specs=out_specs,
            scratch_shapes=[
                pltpu.VMEM((GROUPS, 2 * HB, 2 * (CG + 2) * N4), jnp.bfloat16),
                pltpu.VMEM((4, GROUPS, N2 + QR, TILE), jnp.float32),
            ],
        ),
        out_shape=out_shape,
        compiler_params=pltpu.CompilerParams(vmem_limit_bytes=60 * 2**20),
        cost_estimate=pl.CostEstimate(
            flops=10**10, bytes_accessed=60 * 2**20, transcendentals=0
        ),
        name="split_grids",
    )(scal, weight, grids, *ordered)


def rest_spec(blocks, row_of):
    return pl.BlockSpec(
        (2, 2, 2, blocks, 1, QR, HALF_LANES), lambda i, *_: (0, 0, 0, 0, row_of(i), 0, 0)
    )


def line_spec(row_of):
    return pl.BlockSpec(
        (2, 2, 2, 1, QR, HALF_LANES), lambda i, *_: (0, 0, 0, row_of(i), 0, 0)
    )


def backward_kernel(rows_here, count, scal, *refs):
    used = 19
    c6, c6_next, c6_rest, c6_rest_next, ahead_row, d6, d6_self = refs[:7]
    c5 = dict(zip(SLOTS, refs[7:15]))
    c5_low, c5_high, s5_self, c4 = refs[15:19]
    tables = dict(zip(CASES, refs[used : used + 4]))
    out = refs[used + 4]
    coarse, detail, joined, xb = refs[used + 5 :]
    half_rows = rows_here // 2
    i = pl.program_id(0)
    mine_x = scal[4 * count]
    mine_y = scal[4 * count + 1]
    row = scal[4 * count + 2] + i
    odd = lax.rem(i, 2) == 1
    even = lax.rem(i, 2) == 0

    def one_grid(g, carry):
        level, fine_b, fine_c, fine_d = grid_facts(scal, g)
        active = row < (N1 // 4) * (1 << level)

        def stage(wanted, blocks, source):
            for block in blocks:
                pb, pc, pd = BLOCKS[block]

                @pl.when(active & wanted & (pb <= fine_b) & (pc <= fine_c) & (pd <= fine_d))
                def _(block=block, work=(coarse, detail)[pb], part=2 * pc + pd):
                    for h, sx, sy in SLOTS:
                        quarter = 2 * (sx ^ mine_x) + (sy ^ mine_y)
                        start = pl.multiple_of(quarter * QR, QR)
                        value = source(block, h, sx, sy)
                        for j in range(GROUPS // 2):
                            k = h * (GROUPS // 2) + j
                            work[part, k, pl.ds(start, QR)] = value[:, j * TILE : j * TILE + TILE]

        def here(block, h, sx, sy):
            if block < SHARED_D:
                return c6[h, sx, sy, block, 0]
            return c6_rest[h, sx, sy, block - SHARED_D, 0]

        def between(last):
            def value(block, h, sx, sy):
                if last:
                    after = ahead_row[h, sx, sy, block, 0]
                elif block < SHARED_D:
                    after = c6_next[h, sx, sy, block, 0]
                else:
                    after = c6_rest_next[h, sx, sy, block - SHARED_D, 0]
                mean = 0.5 * (here(block, h, sx, sy) + after)
                if block < SHARED_D:
                    return mean + d6[h, sx, sy, block, 0]
                return mean + d6_self[h, sx, sy, block - SHARED_D, 0]

            return value

        stage((level == 2) & even, range(SHARED_C), here)
        if half_rows > 1:
            stage((level == 2) & odd & (i < rows_here - 1), range(SHARED_C), between(False))
        stage((level == 2) & odd & (i == rows_here - 1), range(SHARED_C), between(True))
        rest = range(SHARED_D, SHARED_C)
        five = level == 1
        stage(five, range(SHARED_D), lambda b, h, x, y: c5[h, x, y][b, 0])
        stage(five & (i < half_rows), rest, lambda b, h, x, y: c5_low[h, x, y, b - SHARED_D, 0])
        stage(five & (i >= half_rows), rest, lambda b, h, x, y: c5_high[h, x, y, b - SHARED_D, 0])
        stage(five, range(SHARED_C, 8), lambda b, h, x, y: s5_self[h, x, y, 0])
        stage(level == 0, range(1), lambda b, h, x, y: c4[h, x, y, 0])

        @pl.when(jnp.logical_not(active))
        def _():
            out[g] = jnp.zeros((1, N2, N3 * N4), jnp.float32)

        for oc, od in CASES:
            for ob in range(2):
                @pl.when(active & (fine_b == ob) & (fine_c == oc) & (fine_d == od))
                def _(oc=oc, od=od, ob=ob):
                    parts = [(pc, pd) for pc in range(oc + 1) for pd in range(od + 1)]
                    ahead = [(0, pd) for pd in range(od + 1)] if oc else []
                    reach = (len(parts) + len(ahead)) * TILE
                    rows = (1 + ob) * HB
                    for place, (pc, pd) in enumerate(parts):
                        part = 2 * pc + pd
                        for k in range(GROUPS):
                            value = coarse[part, k, :HB]
                            if ob:
                                coarse[part, k, HB:] = coarse[part, k, :QR]
                                mean = 0.5 * (value + coarse[part, k, 1 : HB + 1])
                                joined[k, pl.ds(0, HB, stride=2)] = value
                                joined[k, pl.ds(1, HB, stride=2)] = detail[part, k] + mean
                                value = joined[k]
                            for base, piece in zip((0, reach), split_parts(value)):
                                start = base + place * TILE
                                xb[k, :rows, start : start + TILE] = piece
                                if oc and not pc:
                                    start = base + (len(parts) + pd) * TILE
                                    before = (k + GROUPS - 1) % GROUPS
                                    xb[before, :rows, start : start + TILE] = piece
                    table = tables[oc, od][...]
                    lhs = xb[:, :rows, : 2 * reach].reshape(GROUPS * rows, 2 * reach)
                    result = jnp.dot(
                        lhs[:, :reach], table, preferred_element_type=jnp.float32
                    ) + jnp.dot(lhs[:, reach:], table, preferred_element_type=jnp.float32)
                    span = CG * N4 if oc else CG // 2 * N4
                    for k in range(GROUPS):
                        out[g, 0, :rows, k * span : k * span + span] = result[
                            k * rows : k * rows + rows
                        ]
                    if not ob:
                        out[g, 0, HB:, :] = jnp.zeros((HB, N3 * N4), jnp.float32)
                    if not oc:
                        out[g, 0, :, HC * N4 :] = jnp.zeros((N2, HC * N4), jnp.float32)
        return carry

    lax.fori_loop(0, count, one_grid, 0)


def backward(count, scal, rows_here, values):
    half_rows = rows_here // 2
    tables = backward_tables()
    ordered = [tables[case] for case in CASES]

    def constant(table):
        return pl.BlockSpec(table.shape, lambda i, *_: (0, 0))

    rest = SHARED_C - SHARED_D
    c6, c6_rest, ahead_row, d6, d6_self = values[:5]
    operands = [c6, c6, c6_rest, c6_rest, ahead_row, d6, d6_self]
    following = lambda i: jnp.minimum((i + 1) // 2, half_rows - 1)
    in_specs = [
        rest_spec(SHARED_D, lambda i: i // 2),
        rest_spec(SHARED_D, following),
        rest_spec(rest, lambda i: i // 2),
        rest_spec(rest, following),
        rest_spec(SHARED_C, lambda i: 0),
        rest_spec(SHARED_D, lambda i: i // 2),
        rest_spec(rest, lambda i: i // 2),
    ]
    c5, c5_low, c5_high, s5_self = values[5:]
    operands += [c5[slot] for slot in SLOTS] + [c5_low, c5_high, s5_self]
    in_specs += [
        pl.BlockSpec((SHARED_D, 1, QR, HALF_LANES), lambda i, *_: (0, i, 0, 0))
    ] * 8 + [
        rest_spec(rest, lambda i: jnp.minimum(i, half_rows - 1)),
        rest_spec(rest, lambda i: jnp.maximum(i - half_rows, 0)),
        line_spec(lambda i: i),
    ]
    c4 = jnp.stack([c5[slot][SHARED_D] for slot in SLOTS])
    operands.append(c4.reshape((2, 2, 2) + c4.shape[1:]))
    in_specs.append(line_spec(lambda i: i))
    return pl.pallas_call(
        lambda *refs: backward_kernel(rows_here, count, *refs),
        grid_spec=pltpu.PrefetchScalarGridSpec(
            num_scalar_prefetch=1,
            grid=(rows_here,),
            in_specs=in_specs + [constant(table) for table in ordered],
            out_specs=pl.BlockSpec((count, 1, N2, N3 * N4), lambda i, *_: (0, i, 0, 0)),
            scratch_shapes=[
                pltpu.VMEM((4, GROUPS, HB + QR, TILE), jnp.float32),
                pltpu.VMEM((4, GROUPS, HB, TILE), jnp.float32),
                pltpu.VMEM((GROUPS, N2, TILE), jnp.float32),
                pltpu.VMEM((GROUPS, N2, 12 * TILE), jnp.bfloat16),
            ],
        ),
        out_shape=jax.ShapeDtypeStruct((count, rows_here, N2, N3 * N4), jnp.float32),
        compiler_params=pltpu.CompilerParams(vmem_limit_bytes=60 * 2**20),
        cost_estimate=pl.CostEstimate(
            flops=10**10, bytes_accessed=60 * 2**20, transcendentals=0
        ),
        name="join_grids",
    )(scal, *operands, *ordered)


def stack_slots(pieces):
    return jnp.stack(
        [
            jnp.stack([jnp.stack([pieces[h, sx, sy] for sy in range(2)]) for sx in range(2)])
            for h in range(2)
        ]
    )


def exchange(value, axis, domains):
    dom_count = lax.axis_size("dom")
    pairs = []
    for x in range(2):
        for y in range(2):
            other = (1 - x, y) if axis == "half" else (x, 1 - y)
            for d in range(domains):
                pairs.append(
                    ((x * 2 + y) * dom_count + d, (other[0] * 2 + other[1]) * dom_count + d)
                )
    return lax.ppermute(value, ("half", "grid", "dom"), pairs)


def reduce_quarter(pieces, domains):
    reduced = []
    for h in range(2):
        first, second = (("half", "grid"), ("grid", "half"))[h]
        far = lambda a, b: pieces[(h, a, b) if h == 0 else (h, b, a)]
        onward = exchange(far(1, 1), first, domains)
        nearby = exchange(far(1, 0), first, domains)
        onward = far(0, 1) + onward
        nearby = far(0, 0) + nearby
        onward = exchange(onward, second, domains)
        reduced.append(nearby + onward)
    return jnp.stack(reduced)


def gather_quarters(own, domains):
    pieces = {}
    for h in range(2):
        first, second = (("half", "grid"), ("grid", "half"))[h]
        place = lambda a, b: (h, a, b) if h == 0 else (h, b, a)
        pieces[place(0, 0)] = own[h]
        pieces[place(0, 1)] = exchange(own[h], second, domains)
        pieces[place(1, 0)] = exchange(own[h], first, domains)
        pieces[place(1, 1)] = exchange(pieces[place(0, 1)], first, domains)
    return pieces


def rows_up(value, sources):
    half_rows = value.shape[-3] // 2
    low = lax.ppermute(value[..., :half_rows, :, :], "dom", [(d, 2 * d) for d in range(sources)])
    high = lax.ppermute(
        value[..., half_rows:, :, :], "dom", [(d, 2 * d + 1) for d in range(sources)]
    )
    return low + high


def rows_down(value):
    targets = lax.axis_size("dom") // 2
    low = lax.ppermute(value, "dom", [(2 * d, d) for d in range(targets)])
    high = lax.ppermute(value, "dom", [(2 * d + 1, d) for d in range(targets)])
    return jnp.concatenate([low, high], axis=-3)


def next_row(value, devices):
    return lax.ppermute(
        value[..., :1, :, :], "dom", [((d + 1) % devices, d) for d in range(devices)]
    )


def per_device(grids, levels):
    count, rows_here = grids.shape[:2]
    half_rows = rows_here // 2
    half_size = lax.axis_size("half")
    grid_size = lax.axis_size("grid")
    dom_size = lax.axis_size("dom")
    square = half_size == 2 and grid_size == 2
    group = lax.axis_index("half") * grid_size + lax.axis_index("grid")
    weights = combination_weights(levels).astype(jnp.float32)
    lowest = jnp.array(
        [LEV1 - SPANS[0], LEV2 - SPANS[1], LEV3 - SPANS[2], LEV4 - SPANS[3]], dtype=jnp.int32
    )
    offsets = levels - lowest[None, :]
    own_offsets = lax.dynamic_slice_in_dim(offsets, group * count, count, 0)
    own_weights = lax.dynamic_slice_in_dim(weights, group * count, count, 0)
    zero = jnp.zeros((), jnp.int32)
    place = jnp.stack(
        [
            lax.axis_index("half") if square else zero,
            lax.axis_index("grid") if square else zero,
            lax.axis_index("dom") * rows_here,
        ]
    ).astype(jnp.int32)
    scal = jnp.concatenate([own_offsets.reshape(-1), place])
    sources = dom_size // 2
    quarter_devices = dom_size // 4
    parts = forward(grids, scal, own_weights)
    s5 = dict(zip(SLOTS, parts[:8]))
    s5_low, s5_high, s5_self = parts[8:11]
    e6 = dict(zip(SLOTS, parts[11:19]))
    d6 = dict(zip(SLOTS, parts[19:27]))
    e6_rest, d6_self = parts[27:]

    from_low = lax.ppermute(s5_low, "dom", [(d, 2 * d) for d in range(sources)])
    from_high = lax.ppermute(s5_high, "dom", [(d, 2 * d + 1) for d in range(sources)])
    c6_rest = e6_rest + from_low + from_high
    firsts = jnp.concatenate(
        [stack_slots({slot: e6[slot][:, :1] for slot in SLOTS}), e6_rest[..., :1, :, :]], axis=3
    )
    e6_ahead = next_row(firsts, dom_size)
    d6_self = d6_self.at[..., -1:, :, :].add(-0.5 * e6_ahead[:, :, :, SHARED_D:])
    d6 = {
        slot: d6[slot].at[:, -1:].add(-0.5 * e6_ahead[slot][:SHARED_D]) for slot in SLOTS
    }

    if square:
        s5_own = reduce_quarter(s5, sources)
        d6_own = reduce_quarter(d6, dom_size)
        e6_own = reduce_quarter(e6, dom_size)
        rest_own = reduce_quarter({slot: c6_rest[slot] for slot in SLOTS}, dom_size)
    else:
        s5_own, e6_own, d6_own, rest_own = lax.psum(
            (stack_slots(s5), stack_slots(e6), stack_slots(d6), c6_rest), ("half", "grid")
        )
    taken = max(half_rows // 2, 1) + 1
    s4 = s5_own[..., SHARED_D, :, :, :]
    s5_own = s5_own[..., :SHARED_D, :, :, :]
    lines = 0.0
    for r in range(4):
        start = half_rows * r // 2
        sent = s4[..., start : start + taken, :, :]
        if sent.shape[-3] < taken:
            missing = jnp.zeros(s4.shape[:-3] + (taken - sent.shape[-3],) + s4.shape[-2:])
            sent = jnp.concatenate([sent, missing], axis=-3)
        pairs = [(d, 4 * d + r) for d in range(quarter_devices)]
        lines = lines + lax.ppermute(sent, "dom", pairs)
    for r in range(4):
        if half_rows * r // 2 + taken > rows_here:
            pairs = [((d + 1) % quarter_devices, 4 * d + r) for d in range(quarter_devices)]
            top = lax.ppermute(s4[..., :1, :, :], "dom", pairs)
            lines = lines.at[..., -1:, :, :].add(top)
    means = 0.5 * (lines[..., :-1, :, :] + lines[..., 1:, :, :])
    lines = lines[..., :-1, :, :]
    if half_rows > 1:
        lines = jnp.stack([lines, means], axis=-3).reshape(
            lines.shape[:-3] + (half_rows,) + lines.shape[-2:]
        )
    else:
        lines = jnp.where(lax.rem(lax.axis_index("dom"), 2) == 1, means, lines)
    lifted = rows_up(s5_own, sources)
    c6_own = e6_own + lifted
    c6_own = c6_own.at[..., 0, :, :, :].add(lines)
    c5_own = rows_down(c6_own)
    if half_rows > 1:
        pieces = [
            lax.ppermute(
                c6_own[..., :1, ::2, :, :], "dom", [(4 * d + r, d) for d in range(quarter_devices)]
            )
            for r in range(4)
        ]
    else:
        pieces = [
            lax.ppermute(
                c6_own[..., :1, :, :, :], "dom", [(4 * d + r, d) for d in range(quarter_devices)]
            )
            for r in (0, 2)
        ]
    c4_own = jnp.concatenate(pieces, axis=-3)
    c5_own = jnp.concatenate([c5_own, c4_own], axis=-4)
    ahead_own = next_row(
        jnp.concatenate([c6_own[..., :1, :, :], rest_own[..., :1, :, :]], axis=-4), dom_size
    )
    if square:
        d6 = stack_slots(gather_quarters(d6_own, dom_size))
        c6_rest = stack_slots(gather_quarters(rest_own, dom_size))
        c6 = stack_slots(gather_quarters(c6_own, dom_size))
        ahead_row = stack_slots(gather_quarters(ahead_own, dom_size))
        c5 = gather_quarters(c5_own, sources)
    else:
        c6, d6, c6_rest, ahead_row = c6_own, d6_own, rest_own, ahead_own
        c5 = {slot: c5_own[slot] for slot in SLOTS}
    c5_low = lax.ppermute(c6_rest, "dom", [(2 * d, d) for d in range(sources)])
    c5_high = lax.ppermute(c6_rest, "dom", [(2 * d + 1, d) for d in range(sources)])
    values = [c6, c6_rest, ahead_row, d6, d6_self]
    values += [c5, c5_low, c5_high, s5_self]
    return backward(count, scal, rows_here, values)


def solution(mesh):
    return jax.shard_map(
        per_device,
        mesh=mesh,
        in_specs=(P(("half", "grid"), "dom", None, None), P()),
        out_specs=P(("half", "grid"), "dom", None, None),
        check_vma=False,
    )
```
